512 devices in a mesh: member: 16 (over z, core), band: 32 (over y, x).
Axes of the slice: x: 4, y: 8, z: 8, core: 2. Of those that a mesh axis runs over, the one named last changes fastest.
Arguments:
- ensemble: bfloat16 [16, 2, 16, 128, 1440], P('member', None, None, 'band'), may hold values from -6 to 6
- member_weight: float32 [16], replicated, may hold values from 0.5 to 2
- member_of_slot: int32 [16], P('member'), may hold values from 0 to 15, each once
- halfwidth: int32 [16], replicated, may hold values from 1 to 4, as said below
- static_root: float32 [16, 16], replicated, may hold values from -1.5 to 1.5
- innovation: bfloat16 [2, 16, 128, 1440], P(None, None, 'band'), may hold values from -6 to 6
- precision: bfloat16 [16, 128, 1440], P(None, 'band'), may hold values from 0.1 to 3
Outputs:
- control_members: float32 [16, 16, 128, 1440], P('member', None, 'band')
- control_static: float32 [16, 128, 1440], P(None, 'band')
- increment: float32 [2, 16, 128, 1440], P(None, 'member', 'band')
The draws below stay inside these ranges and needn't reach their ends.
Inputs may be any that keep to these rules, and one draw needn't show every extreme that they name: `member_of_slot`: each member appears in exactly one slot. `halfwidth`: some level has a half-width of exactly 4.
All inputs are finite; a program needn't handle non-finite values.
Results may differ from the reference program's by a relative error of at most 0.0062.
Values may be sent and summed in bfloat16 or wider, within the bound.
A program may use at most 64 MiB of HBM per device.

```python
import math
import jax
import jax.numpy as jnp
from jax import lax

LEV = 16
LON = 1440
TSLOT = 2
ITERS = 2
HMAX = 4
LREACH = 18
MEMBERS = 16
LAT = 128


def draw_halfwidth(key, part):
    first_key = jax.random.fold_in(key, 11)
    second_key = jax.random.fold_in(key, 12)
    widths = jax.random.randint(first_key, (LEV,), 1, HMAX + 1, dtype=jnp.int32)
    chosen = jax.random.randint(second_key, (), 0, LEV, dtype=jnp.int32)
    return jnp.where(jnp.arange(LEV, dtype=jnp.int32) == chosen, HMAX, widths).astype(jnp.int32)


def draw_precision(key, part):
    uniform_draw = jax.random.uniform(jax.random.fold_in(key, 21), (LEV, LAT, LON), jnp.float32)
    base = jnp.exp(jnp.log(0.1) * (1.0 - uniform_draw))
    latitude = jnp.arange(LAT, dtype=jnp.float32)[None, :, None]
    factor = 1.0 + 2.0 * latitude / max(LAT - 1, 1)
    return (base * factor).astype(jnp.bfloat16)


def steps_of(rng, extent, shards, smallest, top_value):
    level, own = 1.0, jax.random.fold_in(rng, 6)
    for axis_at, parts in shards:
        steps = jnp.exp(jax.random.uniform(jax.random.fold_in(own, axis_at), (parts,), jnp.float32, smallest / len(shards), top_value / len(shards)))
        level = level * jnp.repeat(steps, extent[axis_at] // parts).reshape([-1 if axis == axis_at else 1 for axis in range(len(extent))])
    return level


def normal_values(stream_key, dims, spread, limit, cuts=(), kind=jnp.bfloat16):
    values = jax.random.normal(stream_key, dims, jnp.float32) * spread
    if len(cuts) > 0:
        values = steps_of(stream_key, dims, cuts, -0.22, 0.18) * values
    return jnp.clip(values, min=-limit, max=limit).astype(kind)


def setup_inputs(seed: int = 0) -> dict:
    arg_keys = jax.random.split(jax.random.key(seed), 8)
    return {
        "ensemble": normal_values(arg_keys[0], (MEMBERS, TSLOT, LEV, LAT, LON), 1.0, 6.0, ((0, 16), (3, 32))),
        "member_weight": jnp.clip(jnp.exp(jax.random.uniform(arg_keys[1], (MEMBERS,), jnp.float32, math.log(0.5), math.log(2.0))), 0.5, 2.0),
        "member_of_slot": jax.random.permutation(arg_keys[2], MEMBERS).astype(jnp.int32),
        "halfwidth": draw_halfwidth(jax.random.fold_in(arg_keys[7], 71), 0),
        "static_root": normal_values(arg_keys[4], (LEV, LEV), LEV ** -0.5, 1.5, (), jnp.float32),
        "innovation": normal_values(arg_keys[5], (TSLOT, LEV, LAT, LON), 1.0, 6.0, ((2, 32),)),
        "precision": draw_precision(jax.random.fold_in(arg_keys[7], 71), 0),
    }


ensemble_share = 0.8
static_share = 0.6
length_scale = 6.0

def lon_kernel(reach, width):
    rows_index = jnp.arange(width + 2 * reach, dtype=jnp.int32)[:, None]
    cols_index = jnp.arange(width, dtype=jnp.int32)[None, :]
    distance = jnp.abs(rows_index - reach - cols_index).astype(jnp.float32)
    values = jnp.exp(-0.5 * (distance / length_scale) ** 2) / (length_scale * math.sqrt(2.0 * math.pi))
    return jnp.where(distance <= reach, values, jnp.zeros_like(values)).astype(jnp.bfloat16)

def smooth_longitude(field, reach, blocks):
    width = field.shape[-1] // blocks
    pieces = field.reshape(field.shape[:-1] + (blocks, width))
    before = jnp.roll(pieces, 1, axis=-2)[..., width - reach:]
    after = jnp.roll(pieces, -1, axis=-2)[..., :reach]
    window = jnp.concatenate([before, pieces, after], axis=-1)
    kernel = lon_kernel(reach, width)
    result = jnp.einsum('...bm,mo->...bo', window.astype(jnp.float32), kernel.astype(jnp.float32))
    return result.reshape(field.shape).astype(jnp.bfloat16)

def taper_weights(halfwidth, reach):
    offsets = jnp.abs(jnp.arange(-reach, reach + 1, dtype=jnp.int32)).astype(jnp.float32)
    spans = halfwidth.astype(jnp.float32)[:, None] + 1.0
    return jnp.maximum(1.0 - offsets[None, :] / spans, 0.0) / spans

def localize(field, taper):
    smoothed = smooth_longitude(field.astype(jnp.bfloat16), LREACH, LON // LREACH)
    padded = jnp.pad(smoothed, ((0, 0), (HMAX, HMAX), (0, 0)))
    row_count = field.shape[1]
    summed = jnp.zeros(field.shape, jnp.float32)
    for offset in range(2 * HMAX + 1):
        summed = summed + taper[:, offset][:, None, None] * padded[:, offset:offset + row_count, :].astype(jnp.float32)
    return summed

def forward(control_members, control_static, scaled, ensemble, taper, static_root):

    def add_member(running, items):
        weight, member_field, control = items
        localized = localize(control, taper)
        return (running + weight * member_field.astype(jnp.float32) * localized[None], None)
    start = jnp.zeros((TSLOT, LEV, LAT, LON), jnp.float32)
    summed, _ = lax.scan(add_member, start, (scaled, ensemble, control_members))
    static = jnp.einsum('lq,qyx->lyx', static_root, control_static, precision=lax.Precision.HIGHEST)
    return ensemble_share * summed + static_share * static[None]

def adjoint(weighted, scaled, ensemble, taper, static_root):

    def one_member(items):
        weight, member_field = items
        folded = weight * lax.optimization_barrier(jnp.sum(member_field.astype(jnp.float32) * weighted, axis=0))
        return ensemble_share * localize(folded, taper)
    grad_members = lax.map(one_member, (scaled, ensemble))
    grad_static = static_share * jnp.einsum('ql,qyx->lyx', static_root, lax.optimization_barrier(jnp.sum(weighted, axis=0)), precision=lax.Precision.HIGHEST)
    return (grad_members, grad_static)

def reference(ensemble, member_weight, member_of_slot, halfwidth, static_root, innovation, precision):
    scaled = member_weight[member_of_slot]
    taper = taper_weights(halfwidth, HMAX)
    precise = precision.astype(jnp.float32)
    res_members, res_static = adjoint(precise[None] * innovation.astype(jnp.float32), scaled, ensemble, taper, static_root)
    dir_members, dir_static = (res_members, res_static)
    sol_members = jnp.zeros_like(res_members)
    sol_static = jnp.zeros_like(res_static)
    increment = jnp.zeros((TSLOT, LEV, LAT, LON), jnp.float32)
    norm_now = jnp.sum(res_members * res_members) + jnp.sum(res_static * res_static)
    for iteration in range(ITERS):
        image = forward(dir_members, dir_static, scaled, ensemble, taper, static_root)
        hes_members, hes_static = adjoint(precise[None] * image, scaled, ensemble, taper, static_root)
        hes_members = dir_members + hes_members
        hes_static = dir_static + hes_static
        alpha = norm_now / (jnp.sum(dir_members * hes_members) + jnp.sum(dir_static * hes_static))
        sol_members = sol_members + alpha * dir_members
        sol_static = sol_static + alpha * dir_static
        increment = increment + alpha * image
        res_members = res_members - alpha * hes_members
        res_static = res_static - alpha * hes_static
        norm_next = jnp.sum(res_members * res_members) + jnp.sum(res_static * res_static)
        ratio = norm_next / norm_now
        dir_members = res_members + ratio * dir_members
        dir_static = res_static + ratio * dir_static
        norm_now = norm_next
    return (sol_members, sol_static, increment)
```

```python
import functools
import math

import jax
import jax.numpy as jnp
import numpy as np
from jax import lax
from jax.experimental import pallas as pl
from jax.experimental.pallas import tpu as pltpu
from jax.sharding import PartitionSpec as P

HMAX = 4
LREACH = 18
TILE = 256
EDGE = 128

ensemble_share = 0.8
static_share = 0.6
length_scale = 6.0
MESH = pl.DeviceIdType.MESH


def window_weights(width, padded):
    tiles = padded // TILE
    kinds = []
    for tile in (0, 1, tiles - 1):
        start = tile * TILE
        rows = np.arange(start - EDGE, start + TILE + EDGE)
        if tile == 0:
            rows[:EDGE] = np.arange(padded - EDGE, padded)
        if tile == tiles - 1:
            rows[-EDGE:] = np.arange(EDGE)
        cols = np.arange(start, start + TILE)
        apart = np.abs(rows[:, None] - cols[None, :])
        apart = np.minimum(apart, width - apart)
        near = (apart <= LREACH) & (rows[:, None] < width) & (cols[None, :] < width)
        distance = apart.astype(np.float32)
        values = np.exp(-0.5 * (distance / np.float32(length_scale)) ** 2) / np.float32(
            length_scale * math.sqrt(2.0 * math.pi)
        )
        kinds.append(np.where(near, values, 0.0).astype(np.float32))
    return np.stack(kinds)


def halves(matrix):
    high = lax.reduce_precision(matrix, 8, 7)
    return jnp.stack([high, matrix - high]).astype(jnp.bfloat16)


def mul(a, b):
    return jnp.dot(a, b, preferred_element_type=jnp.float32)


def mul_wide(weights, field):
    high = field.astype(jnp.bfloat16)
    low = (field - high.astype(jnp.float32)).astype(jnp.bfloat16)
    return mul(weights[0], high) + mul(weights[0], low) + mul(weights[1], high)


def kernel(
    members, bands, across, tiles,
    ens_ref, w0_ref, p_ref, t1_ref, t2_ref, c1_ref, c2_ref, sel_ref, krt_ref, krm_ref, wk_ref,
    outm_ref, outs_ref, inc_ref,
    x_ref, s_ref, hp_ref, hn_ref, part_ref, rs_ref, gown_ref, gall_ref,
    r0_ref, r1_ref, r0s_ref, r1s_ref, im0_ref, im1_ref,
    vec_ref, tot_ref, allm_ref, allx_ref, ally_ref,
    h_send, h_recv, rs_send, rs_recv, g_send, g_recv, m_send, m_recv, x_send, x_recv, y_send, y_recv,
):
    m = lax.axis_index("member")
    band = lax.axis_index("band")
    up = bands // across
    by = band // across
    bx = lax.rem(band, across)
    levels = gall_ref.shape[0]
    eight = gall_ref.shape[1]
    rows2 = levels * eight
    rows1 = rows2 // 2

    def at_m(o):
        return lax.rem(m + o, members)

    def at_band(o):
        return lax.rem(band + o, bands)

    def x_peer(o):
        return lax.rem(bx + o, across)

    def y_peer(o):
        return lax.rem(by + o, up)

    barrier = pltpu.get_barrier_semaphore()
    greeted = 0
    for o in range(1, members):
        pl.semaphore_signal(
            barrier, inc=1, device_id=(at_m(o), band), device_id_type=MESH
        )
        greeted += 1
    others = [at_band(1), at_band(bands - 1)]
    others += [by * across + x_peer(o) for o in range(1, across)]
    others += [y_peer(o) * across + bx for o in range(1, up)]
    for other in others:
        pl.semaphore_signal(barrier, inc=1, device_id=(m, other), device_id_type=MESH)
        greeted += 1
    pl.semaphore_wait(barrier, greeted)

    sends = []

    def push(src, dst, send, recv, member, other):
        copy = pltpu.make_async_remote_copy(
            src_ref=src, dst_ref=dst, send_sem=send, recv_sem=recv,
            device_id=(member, other), device_id_type=MESH,
        )
        copy.start()
        sends.append(copy)
        return copy

    def arrived(like, dst, send, recv, member, other):
        pltpu.make_async_remote_copy(
            src_ref=like, dst_ref=dst, send_sem=send, recv_sem=recv,
            device_id=(member, other), device_id_type=MESH,
        ).wait_recv()

    def columns(i):
        return pl.ds(pl.multiple_of(i * TILE, TILE), TILE)

    def over_tiles(body, init=None):
        if init is None:
            def step(i, carry):
                body(columns(i))
                return carry
            lax.fori_loop(0, tiles, step, 0)
            return None
        return lax.fori_loop(0, tiles, lambda i, carry: body(columns(i), carry), init)

    def smooth(phase):
        out = s_ref.at[phase]
        last = tiles * TILE
        first = jnp.concatenate(
            [x_ref[:, last - EDGE : last], x_ref[:, : TILE + EDGE]], axis=1
        )
        out[:, :TILE] = mul(first, wk_ref[0]).astype(jnp.bfloat16)

        def inner(i, carry):
            start = pl.multiple_of(i * TILE - EDGE, EDGE)
            window = x_ref[:, pl.ds(start, TILE + 2 * EDGE)]
            out[:, columns(i)] = mul(window, wk_ref[1]).astype(jnp.bfloat16)
            return carry

        lax.fori_loop(1, tiles - 1, inner, 0)
        final = jnp.concatenate(
            [x_ref[:, last - TILE - EDGE : last], x_ref[:, :EDGE]], axis=1
        )
        out[:, last - TILE : last] = mul(final, wk_ref[2]).astype(jnp.bfloat16)

    def send_halo(phase):
        up_copy = push(
            s_ref.at[phase], hp_ref.at[phase], h_send.at[phase, 0], h_recv.at[phase, 0],
            m, at_band(1),
        )
        down_copy = push(
            s_ref.at[phase], hn_ref.at[phase], h_send.at[phase, 1], h_recv.at[phase, 1],
            m, at_band(bands - 1),
        )
        return up_copy, down_copy

    def stacked(phase, cols):
        return jnp.concatenate(
            [hp_ref[phase, :, cols], s_ref[phase, :, cols], hn_ref[phase, :, cols]], axis=0
        )

    def fold(cols, field):
        products = (ens_ref[:, cols] * field).reshape(levels, eight, TILE)
        both = (products + pltpu.roll(products, eight // 2, 1)).reshape(rows2, TILE)
        x_ref[:, cols] = mul(sel_ref[...], both.astype(jnp.bfloat16)).astype(jnp.bfloat16)

    def image(phase, stage, static_ref, out):
        def partial(cols):
            localized = mul(t2_ref[...], stacked(phase, cols)) * c2_ref[...]
            products = (localized * ens_ref[:, cols]).reshape(levels, eight, TILE)
            part_ref[stage, :, :, cols] = products.astype(jnp.bfloat16)

        over_tiles(partial)
        copies = []
        for o in range(1, members):
            copies.append(push(
                part_ref.at[stage, at_m(o)], rs_ref.at[stage, o - 1],
                rs_send.at[stage, o - 1], rs_recv.at[stage, o - 1], at_m(o), band,
            ))

        def static(cols):
            out[:, cols] = static_share * mul_wide(krm_ref, static_ref[:, cols])

        over_tiles(static)
        for copy in copies:
            copy.wait_recv()

        def collect(cols):
            out[:, cols] = (
                out[:, cols]
                + part_ref[stage, m, :, cols].astype(jnp.float32)
                + jnp.sum(rs_ref[stage, :, :, cols].astype(jnp.float32), axis=0)
            )

        over_tiles(collect)

    def squares(a, b):
        return jnp.sum((a * b).reshape(rows1 // 8, 8, TILE), axis=0)

    def total_of(acc):
        return jnp.sum(jnp.sum(acc, axis=1, keepdims=True), axis=0, keepdims=True)

    def pack(values):
        row = lax.broadcasted_iota(jnp.int32, (8, 128), 0)
        packed = jnp.zeros((8, 128), jnp.float32)
        for at, value in enumerate(values):
            packed = jnp.where(row == at, value, packed)
        return packed

    def gather_start(k, stage, value, table, count, own, peer, send, recv):
        vec_ref[k, stage] = value
        table[k, own] = value
        for o in range(1, count):
            member, other = peer(o)
            push(
                vec_ref.at[k, stage], table.at[k, own], send.at[k, o - 1], recv.at[k, o - 1],
                member, other,
            )

    def gather_wait(k, stage, table, count, source, peer, send, recv):
        for o in range(1, count):
            member, other = peer(o)
            arrived(
                vec_ref.at[k, stage], table.at[k, source(o)], send.at[k, o - 1],
                recv.at[k, o - 1], member, other,
            )
        return jnp.sum(table[k], axis=0)

    def m_to(o):
        return at_m(o), band

    def x_to(o):
        return m, by * across + x_peer(o)

    def y_to(o):
        return m, y_peer(o) * across + bx

    def m_start(k, value):
        gather_start(k, 0, value, allm_ref, members, m, m_to, m_send, m_recv)

    def m_wait(k):
        return gather_wait(k, 0, allm_ref, members, lambda o: at_m(members - o), m_to, m_send, m_recv)

    def x_start(k, value):
        gather_start(k, 1, value, allx_ref, across, bx, x_to, x_send, x_recv)

    def x_wait(k):
        return gather_wait(k, 1, allx_ref, across, lambda o: x_peer(across - o), x_to, x_send, x_recv)

    def y_start(k, value):
        gather_start(k, 2, value, ally_ref, up, by, y_to, y_send, y_recv)

    def y_wait(k):
        return gather_wait(k, 2, ally_ref, up, lambda o: y_peer(up - o), y_to, y_send, y_recv)

    over_tiles(lambda cols: fold(cols, w0_ref[:, cols]))
    smooth(0)
    copies = send_halo(0)

    def first_static(cols, acc):
        value = static_share * mul_wide(krt_ref, w0_ref[:, cols])
        r0s_ref[:, cols] = value
        return acc + squares(value, value)

    zero = jnp.zeros((8, TILE), jnp.float32)
    rr_static = over_tiles(first_static, zero)
    for copy in copies:
        copy.wait_recv()

    def first_members(cols, acc):
        value = mul(t1_ref[...], stacked(0, cols)) * c1_ref[...]
        r0_ref[:, cols] = value
        x_ref[:, cols] = value.astype(jnp.bfloat16)
        return acc + squares(value, value)

    rr_members = over_tiles(first_members, zero)

    smooth(1)
    copies = send_halo(1)
    for copy in copies:
        copy.wait_recv()
    image(1, 0, r0s_ref, im0_ref)

    def weigh(cols, acc):
        value = im0_ref[:, cols]
        weighted = p_ref[:, cols] * value
        gown_ref[:, cols] = weighted.astype(jnp.bfloat16)
        return acc + weighted * value

    q00 = over_tiles(weigh, zero)
    gall_ref[m] = gown_ref[...]
    for o in range(1, members):
        push(gown_ref, gall_ref.at[m], g_send.at[o - 1], g_recv.at[o - 1], at_m(o), band)
    m_start(0, pack([total_of(rr_members + rr_static * (1.0 / members)), total_of(q00)]))
    for o in range(1, members):
        arrived(
            gown_ref, gall_ref.at[at_m(members - o)], g_send.at[o - 1], g_recv.at[o - 1],
            at_m(o), band,
        )

    def gathered(cols):
        return gall_ref[:, :, cols].astype(jnp.float32).reshape(rows2, TILE)

    over_tiles(lambda cols: fold(cols, gathered(cols)))
    x_start(0, m_wait(0))
    smooth(2)
    copies = send_halo(2)

    y_start(0, x_wait(0))

    def second_static(cols):
        field = gathered(cols).astype(jnp.bfloat16)
        r1s_ref[:, cols] = r0s_ref[:, cols] + static_share * (
            mul(krt_ref[0], field) + mul(krt_ref[1], field)
        )

    over_tiles(second_static)
    tot_ref[0] = y_wait(0)
    rr0 = tot_ref[0, 0:1, 0:1]
    q00 = tot_ref[0, 1:2, 0:1]
    alpha0 = rr0 / (rr0 + q00)
    for copy in copies:
        copy.wait_recv()

    def second_residual(cols, acc):
        rr, cross = acc
        first = r0_ref[:, cols]
        hessian = first + mul(t1_ref[...], stacked(2, cols)) * c1_ref[...]
        value = first - alpha0 * hessian
        r1_ref[:, cols] = value
        x_ref[:, cols] = value.astype(jnp.bfloat16)
        return rr + squares(value, value), cross + squares(value, first)

    rr_members, cross_members = over_tiles(second_residual, (zero, zero))
    smooth(3)
    copies = send_halo(3)

    def second_static_residual(cols, acc):
        rr, cross = acc
        first = r0s_ref[:, cols]
        value = first - alpha0 * r1s_ref[:, cols]
        r1s_ref[:, cols] = value
        return rr + squares(value, value), cross + squares(value, first)

    rr_static, cross_static = over_tiles(second_static_residual, (zero, zero))
    for copy in copies:
        copy.wait_recv()
    image(3, 1, r1s_ref, im1_ref)

    def second_sums(cols, acc):
        q11, q01 = acc
        value = im1_ref[:, cols]
        weighted = p_ref[:, cols] * value
        return q11 + weighted * value, q01 + weighted * im0_ref[:, cols]

    q11, q01 = over_tiles(second_sums, (zero, zero))
    share = 1.0 / members
    m_start(1, pack([
        total_of(rr_members + rr_static * share),
        total_of(cross_members + cross_static * share),
        total_of(q11),
        total_of(q01),
    ]))
    x_start(1, m_wait(1))
    y_start(1, x_wait(1))
    tot_ref[1] = y_wait(1)
    rr1 = tot_ref[1, 0:1, 0:1]
    cross = tot_ref[1, 1:2, 0:1]
    q11 = tot_ref[1, 2:3, 0:1]
    q01 = tot_ref[1, 3:4, 0:1]
    beta = rr1 / rr0
    length = rr1 + beta * (2.0 * cross + beta * rr0)
    curvature = length + q11 + beta * (2.0 * q01 + beta * q00)
    alpha1 = rr1 / curvature
    ahead = alpha0 + alpha1 * beta

    def finish(cols):
        outm_ref[:, cols] = ahead * r0_ref[:, cols] + alpha1 * r1_ref[:, cols]
        outs_ref[:, cols] = ahead * r0s_ref[:, cols] + alpha1 * r1s_ref[:, cols]
        inc_ref[:, cols] = ahead * im0_ref[:, cols] + alpha1 * im1_ref[:, cols]

    over_tiles(finish)
    for copy in sends:
        copy.wait_send()


def shards(ensemble, member_weight, member_of_slot, halfwidth, static_root, innovation, precision):
    f32, bf16 = jnp.float32, jnp.bfloat16
    _, slots, levels, rows, width = ensemble.shape
    members = lax.axis_size("member")
    bands = lax.axis_size("band")
    band = lax.axis_index("band")
    me = lax.axis_index("member")
    across = 4 if bands % 4 == 0 else 1
    up = bands // across
    padded = -(-width // TILE) * TILE
    tiles = padded // TILE
    eight = slots * rows
    rows1, rows2 = levels * rows, levels * eight

    def flat(field):
        field = jnp.transpose(field, (1, 0, 2, 3))
        field = jnp.pad(field, ((0, 0), (0, 0), (0, 0), (0, padded - width)))
        return field.reshape(rows2, padded)

    picker = member_of_slot == jnp.arange(members, dtype=jnp.int32)
    scaled = jnp.sum(jnp.where(picker, member_weight, 0.0))
    precise = precision.astype(f32)
    ens = flat(ensemble[0].astype(f32) * scaled)
    w0 = flat(innovation.astype(f32) * precise[None])
    own = lax.dynamic_slice_in_dim(precise, me, 1, 0)[0]
    own = jnp.pad(jnp.concatenate([own] * slots, axis=0), ((0, 0), (0, padded - width)))

    lev1 = np.repeat(np.arange(levels), rows)
    row1 = np.tile(np.arange(rows), levels)
    lev2 = np.repeat(np.arange(levels), eight)
    row2 = np.tile(np.arange(rows), levels * slots)
    lev3 = np.tile(lev1, 3)
    row3 = np.concatenate([row1 - rows, row1, row1 + rows])
    side = np.repeat(np.arange(3), rows1)
    spans = halfwidth.astype(f32) + 1.0
    inside = jnp.where(
        side == 0, band > 0, jnp.where(side == 2, band < bands - 1, True)
    )

    def taper(lev, row):
        span = jnp.repeat(spans, len(lev) // levels)[:, None]
        offsets = np.abs(row3[None, :] - row[:, None]).astype(np.float32)
        same = lev[:, None] == lev3[None, :]
        weights = jnp.maximum(span - offsets, 0.0)
        weights = jnp.where(same & inside[None, :], weights, 0.0).astype(bf16)
        return weights, ensemble_share / (span * span)

    t1, c1 = taper(lev1, row1)
    t2, c2 = taper(lev2, row2)
    slot2 = np.tile(np.repeat(np.arange(slots), rows), levels)
    same12 = (row1[:, None] == row2[None, :]).astype(np.float32)
    sel = jnp.asarray(
        same12 * (lev1[:, None] == lev2[None, :]) * (slot2[None, :] == 0), bf16
    )
    krt = jnp.repeat(jnp.repeat(static_root.T, rows, 0), eight, 1) * same12
    root_row = lax.dynamic_slice_in_dim(static_root, me, 1, 0)
    rowe = np.tile(np.arange(rows), slots)
    krm = jnp.repeat(root_row, rows, 1) * (rowe[:, None] == row1[None, :])
    weights = jnp.asarray(window_weights(width, padded), bf16)

    vmem = pl.BlockSpec(memory_space=pltpu.VMEM)
    dma = pltpu.SemaphoreType.DMA
    outm, outs, inc = pl.pallas_call(
        functools.partial(kernel, members, bands, across, tiles),
        out_shape=[
            jax.ShapeDtypeStruct((rows1, padded), f32),
            jax.ShapeDtypeStruct((rows1, padded), f32),
            jax.ShapeDtypeStruct((eight, padded), f32),
        ],
        in_specs=[vmem] * 11,
        out_specs=[vmem] * 3,
        scratch_shapes=[
            pltpu.VMEM((rows1, padded), bf16),
            pltpu.VMEM((4, rows1, padded), bf16),
            pltpu.VMEM((4, rows1, padded), bf16),
            pltpu.VMEM((4, rows1, padded), bf16),
            pltpu.VMEM((2, levels, eight, padded), bf16),
            pltpu.VMEM((2, members - 1, eight, padded), bf16),
            pltpu.VMEM((eight, padded), bf16),
            pltpu.VMEM((levels, eight, padded), bf16),
            pltpu.VMEM((rows1, padded), f32),
            pltpu.VMEM((rows1, padded), f32),
            pltpu.VMEM((rows1, padded), f32),
            pltpu.VMEM((rows1, padded), f32),
            pltpu.VMEM((eight, padded), f32),
            pltpu.VMEM((eight, padded), f32),
            pltpu.VMEM((2, 3, 8, 128), f32),
            pltpu.VMEM((2, 8, 128), f32),
            pltpu.VMEM((2, members, 8, 128), f32),
            pltpu.VMEM((2, across, 8, 128), f32),
            pltpu.VMEM((2, up, 8, 128), f32),
            dma((4, 2)),
            dma((4, 2)),
            dma((2, members - 1)),
            dma((2, members - 1)),
            dma((members - 1,)),
            dma((members - 1,)),
            dma((2, members - 1)),
            dma((2, members - 1)),
            dma((2, max(across - 1, 1))),
            dma((2, max(across - 1, 1))),
            dma((2, max(up - 1, 1))),
            dma((2, max(up - 1, 1))),
        ],
        compiler_params=pltpu.CompilerParams(collective_id=0, has_side_effects=True),
    )(ens, w0, own, t1, t2, c1, c2, sel, halves(krt), halves(krm), weights)
    control = outm[:, :width].reshape(1, levels, rows, width)
    static = outs[:, :width].reshape(levels, rows, width)
    increment = inc[:, :width].reshape(slots, 1, rows, width)
    return control, static, increment


def solution(mesh):
    return jax.shard_map(
        shards,
        mesh=mesh,
        in_specs=(
            P("member", None, None, "band", None),
            P(),
            P("member"),
            P(),
            P(),
            P(None, None, "band", None),
            P(None, "band", None),
        ),
        out_specs=(
            P("member", None, "band", None),
            P(None, "band", None),
            P(None, "member", "band", None),
        ),
        check_vma=False,
    )
```

```python
import functools
import math

import jax
import jax.numpy as jnp
import numpy as np
from jax import lax
from jax.experimental import pallas as pl
from jax.experimental.pallas import tpu as pltpu
from jax.sharding import PartitionSpec as P

HMAX = 4
LREACH = 18
TILE = 256
EDGE = 128

ensemble_share = 0.8
static_share = 0.6
length_scale = 6.0
MESH = pl.DeviceIdType.MESH


def window_weights(width, padded):
    tiles = padded // TILE
    kinds = []
    for tile in (0, 1, tiles - 1):
        start = tile * TILE
        rows = np.arange(start - EDGE, start + TILE + EDGE)
        if tile == 0:
            rows[:EDGE] = np.arange(padded - EDGE, padded)
        if tile == tiles - 1:
            rows[-EDGE:] = np.arange(EDGE)
        cols = np.arange(start, start + TILE)
        apart = np.abs(rows[:, None] - cols[None, :])
        apart = np.minimum(apart, width - apart)
        near = (apart <= LREACH) & (rows[:, None] < width) & (cols[None, :] < width)
        distance = apart.astype(np.float32)
        values = np.exp(-0.5 * (distance / np.float32(length_scale)) ** 2) / np.float32(
            length_scale * math.sqrt(2.0 * math.pi)
        )
        kinds.append(np.where(near, values, 0.0).astype(np.float32))
    return np.stack(kinds)


def mul(a, b):
    return jnp.dot(a, b, preferred_element_type=jnp.float32)


def mul_wide(weights, field):
    high = field.astype(jnp.bfloat16)
    low = (field - high.astype(jnp.float32)).astype(jnp.bfloat16)
    return mul(weights[0], high) + mul(weights[0], low) + mul(weights[1], high)


def kernel(
    members, bands, across, tiles, groups,
    weight_ref, slot_ref, half_ref,
    ens_ref, w0_ref, p_ref, root_ref, wk_ref,
    outm_ref, outs_ref, inc_ref,
    t1_ref, t2_ref, c1_ref, c2_ref, sel_ref, krt_ref, krm_ref,
    x_ref, s_ref, hp_ref, hn_ref, part_ref, rs_ref, gown_ref, gall_ref,
    r0_ref, r1_ref, r0s_ref, r1s_ref, im0_ref, im1_ref,
    vec_ref, tot_ref, allm_ref, allx_ref, ally_ref,
    h_send, h_recv, rs_send, rs_recv, g_send, g_recv, m_send, m_recv, x_send, x_recv, y_send, y_recv,
):
    f32, bf16 = jnp.float32, jnp.bfloat16
    m = lax.axis_index("member")
    band = lax.axis_index("band")
    up = bands // across
    by = band // across
    bx = lax.rem(band, across)
    levels, eight = gall_ref.shape[0], gall_ref.shape[1]
    rows = eight // 2
    rows1, rows2 = levels * rows, levels * eight
    each = levels // groups
    small, large = each * rows, each * eight
    my_group = lax.rem(m, groups)
    my_place = m // groups

    def at_m(o):
        return lax.rem(m + o, members)

    def at_band(o):
        return lax.rem(band + o, bands)

    def x_peer(o):
        return lax.rem(bx + o, across)

    def y_peer(o):
        return lax.rem(by + o, up)

    def place(level):
        return lax.rem(level, groups) * each + level // groups

    barrier = pltpu.get_barrier_semaphore()
    greeted = 0
    for o in range(1, members):
        pl.semaphore_signal(
            barrier, inc=1, device_id=(at_m(o), band), device_id_type=MESH
        )
        greeted += 1
    others = [at_band(1), at_band(bands - 1)]
    others += [by * across + x_peer(o) for o in range(1, across)]
    others += [y_peer(o) * across + bx for o in range(1, up)]
    for other in others:
        pl.semaphore_signal(barrier, inc=1, device_id=(m, other), device_id_type=MESH)
        greeted += 1

    def iota(shape, axis):
        return lax.broadcasted_iota(jnp.int32, shape, axis)

    def over(index, size):
        return lax.shift_right_logical(index, size.bit_length() - 1)

    def level_of(index, height):
        inside = index & (each * height - 1)
        return over(inside, height) * groups + over(index, each * height)

    def span_of(level):
        span = jnp.zeros(level.shape, jnp.int32)
        for at in range(levels):
            span = jnp.where(level == at, half_ref[at] + 1, span)
        return span

    low_side = jnp.where(band > 0, 1, 0)
    high_side = jnp.where(band < bands - 1, 1, 0)
    scaled = jnp.float32(0.0)
    for at in range(members):
        scaled = scaled + jnp.where(slot_ref[0] == at, weight_ref[at], 0.0)

    def taper(height, out, factors, extra):
        shape = (levels * height, 3 * small)
        line, col = iota(shape, 0), iota(shape, 1)
        side = jnp.where(col >= small, 1, 0) + jnp.where(col >= 2 * small, 1, 0)
        within = col - side * small
        apart = jnp.abs((within & (rows - 1)) + (side - 1) * rows - (line & (rows - 1)))
        same = over(within, rows) == over(line & (each * height - 1), height)
        seen = jnp.where(side == 0, low_side, jnp.where(side == 2, high_side, 1)) == 1
        span = span_of(level_of(line, height))
        values = jnp.where(same & seen, jnp.maximum(span - apart, 0), 0)
        out[...] = values.astype(f32).astype(bf16)
        spans = span_of(level_of(iota(factors.shape, 0), height)).astype(f32)
        factors[...] = extra / (spans * spans)

    taper(rows, t1_ref, c1_ref, ensemble_share)
    taper(eight, t2_ref, c2_ref, ensemble_share * scaled)

    def ones(condition):
        return jnp.where(condition, 1.0, 0.0).astype(f32)

    line, col = iota((small, large), 0), iota((small, large), 1)
    picked = over(line, rows) * eight + (line & (rows - 1))
    sel_ref[...] = ones(col == picked).astype(bf16)
    shape = (rows1, levels)
    place1 = ones(level_of(iota(shape, 0), rows) == iota(shape, 1)).astype(bf16)
    shape = (levels, rows2)
    level2 = ones(level_of(iota(shape, 1), eight) == iota(shape, 0)).astype(bf16)
    shape = (levels, rows1)
    level1 = ones(level_of(iota(shape, 1), rows) == iota(shape, 0)).astype(bf16)
    shape = (eight, levels)
    mine = ones(iota(shape, 1) == m).astype(bf16)
    shape = (rows1, rows2)
    match = ones((iota(shape, 0) & (rows - 1)) == (iota(shape, 1) & (rows - 1)))
    shape = (eight, rows1)
    match_row = ones((iota(shape, 0) & (rows - 1)) == (iota(shape, 1) & (rows - 1)))
    root = root_ref[...]
    root_high = root.astype(bf16)
    root_low = (root - root_high.astype(f32)).astype(bf16)
    for at, piece in enumerate((root_high, root_low)):
        spread = lax.dot_general(
            place1, piece, (((1,), (1,)), ((), ())), preferred_element_type=f32
        )
        krt_ref[at] = (mul(spread.astype(bf16), level2) * match).astype(bf16)
        spread = mul(mine, piece)
        krm_ref[at] = (mul(spread.astype(bf16), level1) * match_row).astype(bf16)

    sends = []

    def push(src, dst, send, recv, member, other):
        copy = pltpu.make_async_remote_copy(
            src_ref=src, dst_ref=dst, send_sem=send, recv_sem=recv,
            device_id=(member, other), device_id_type=MESH,
        )
        copy.start()
        sends.append(copy)
        return copy

    def arrived(like, dst, send, recv, member, other):
        pltpu.make_async_remote_copy(
            src_ref=like, dst_ref=dst, send_sem=send, recv_sem=recv,
            device_id=(member, other), device_id_type=MESH,
        ).wait_recv()

    def columns(i):
        return pl.ds(pl.multiple_of(i * TILE, TILE), TILE)

    def over_tiles(body, init=None):
        if init is None:
            def step(i, carry):
                body(columns(i))
                return carry
            lax.fori_loop(0, tiles, step, 0)
            return None
        return lax.fori_loop(0, tiles, lambda i, carry: body(columns(i), carry), init)

    every = [slice(i * TILE, (i + 1) * TILE) for i in range(tiles)]
    last = tiles * TILE

    def smooth(phase, g):
        for i, cols in enumerate(every):
            start, stop = i * TILE - EDGE, (i + 1) * TILE + EDGE
            if i == 0:
                window = jnp.concatenate([x_ref[g, :, last - EDGE :], x_ref[g, :, :stop]], axis=1)
            elif i == tiles - 1:
                window = jnp.concatenate([x_ref[g, :, start:], x_ref[g, :, :EDGE]], axis=1)
            else:
                window = x_ref[g, :, start:stop]
            kind = 0 if i == 0 else 2 if i == tiles - 1 else 1
            s_ref[phase, g, :, cols] = mul(window, wk_ref[kind]).astype(bf16)

    def send_halo(phase, g):
        return (
            push(
                s_ref.at[phase, g], hp_ref.at[phase, g], h_send.at[phase, g, 0],
                h_recv.at[phase, g, 0], m, at_band(1),
            ),
            push(
                s_ref.at[phase, g], hn_ref.at[phase, g], h_send.at[phase, g, 1],
                h_recv.at[phase, g, 1], m, at_band(bands - 1),
            ),
        )

    def small_of(g):
        return slice(g * small, (g + 1) * small)

    def large_of(g):
        return slice(g * large, (g + 1) * large)

    def stacked(phase, g, cols):
        return jnp.concatenate(
            [hp_ref[phase, g, :, cols], s_ref[phase, g, :, cols], hn_ref[phase, g, :, cols]],
            axis=0,
        )

    def fold(g, field):
        for cols in every:
            products = (ens_ref[large_of(g), cols] * field(g, cols)).reshape(each, eight, TILE)
            both = (products + pltpu.roll(products, rows, 1)) * scaled
            both = both.reshape(large, TILE).astype(bf16)
            x_ref[g, :, cols] = mul(sel_ref[...], both).astype(bf16)

    def squares(a, b):
        product = a * b
        return jnp.sum(product.reshape(product.shape[0] // 8, 8, TILE), axis=0)

    def image(phase, stage, static_ref, out, halos):
        def static(cols):
            out[:, cols] = static_share * mul_wide(krm_ref, static_ref[:, cols])

        over_tiles(static)
        for g in range(groups):
            for copy in halos[g]:
                copy.wait_recv()
            for cols in every:
                localized = mul(t2_ref[large_of(g)], stacked(phase, g, cols))
                products = localized * c2_ref[large_of(g), 0:1] * ens_ref[large_of(g), cols]
                part_ref[stage, g * each : (g + 1) * each, :, cols] = products.reshape(
                    each, eight, TILE
                ).astype(bf16)
            for o in range(each):
                there = lax.rem(my_place + o, each)
                copy = pltpu.make_async_remote_copy(
                    src_ref=part_ref.at[stage, g * each + there], dst_ref=rs_ref.at[stage, m],
                    send_sem=rs_send.at[stage, g * each + o], recv_sem=rs_recv.at[stage, m],
                    device_id=(there * groups + g, band), device_id_type=MESH,
                )
                if o > 0:
                    copy.start()
                    sends.append(copy)
                else:
                    pl.when(my_group != g)(copy.start)
                    later.append((my_group != g, copy))
        rs_ref[stage, m] = part_ref[stage, place(m)]
        for o in range(1, members):
            source = at_m(members - o)
            arrived(
                part_ref.at[stage, 0], rs_ref.at[stage, source], rs_send.at[stage, 0],
                rs_recv.at[stage, source], at_m(o), band,
            )

        def collect(cols):
            out[:, cols] = out[:, cols] + jnp.sum(rs_ref[stage, :, :, cols].astype(f32), axis=0)

        over_tiles(collect)

    later = []

    def total_of(acc):
        return jnp.sum(jnp.sum(acc, axis=1, keepdims=True), axis=0, keepdims=True)

    def pack(values):
        line = iota((8, 128), 0)
        packed = jnp.zeros((8, 128), f32)
        for at, value in enumerate(values):
            packed = jnp.where(line == at, value, packed)
        return packed

    def gather_start(k, stage, value, table, count, own, peer, send, recv):
        vec_ref[k, stage] = value
        table[k, own] = value
        for o in range(1, count):
            member, other = peer(o)
            push(
                vec_ref.at[k, stage], table.at[k, own], send.at[k, o - 1], recv.at[k, o - 1],
                member, other,
            )

    def gather_wait(k, stage, table, count, source, peer, send, recv):
        for o in range(1, count):
            member, other = peer(o)
            arrived(
                vec_ref.at[k, stage], table.at[k, source(o)], send.at[k, o - 1],
                recv.at[k, o - 1], member, other,
            )
        return jnp.sum(table[k], axis=0)

    def m_to(o):
        return at_m(o), band

    def x_to(o):
        return m, by * across + x_peer(o)

    def y_to(o):
        return m, y_peer(o) * across + bx

    def m_start(k, value):
        gather_start(k, 0, value, allm_ref, members, m, m_to, m_send, m_recv)

    def m_wait(k):
        return gather_wait(k, 0, allm_ref, members, lambda o: at_m(members - o), m_to, m_send, m_recv)

    def x_start(k, value):
        gather_start(k, 1, value, allx_ref, across, bx, x_to, x_send, x_recv)

    def x_wait(k):
        return gather_wait(k, 1, allx_ref, across, lambda o: x_peer(across - o), x_to, x_send, x_recv)

    def y_start(k, value):
        gather_start(k, 2, value, ally_ref, up, by, y_to, y_send, y_recv)

    def y_wait(k):
        return gather_wait(k, 2, ally_ref, up, lambda o: y_peer(up - o), y_to, y_send, y_recv)

    halos = []
    for g in range(groups):
        fold(g, lambda g, cols: w0_ref[large_of(g), cols])
        smooth(0, g)
        if g == 0:
            pl.semaphore_wait(barrier, greeted)
        halos.append(send_halo(0, g))

    def first_static(cols, acc):
        value = static_share * mul_wide(krt_ref, w0_ref[:, cols])
        r0s_ref[:, cols] = value
        return acc + squares(value, value)

    zero = jnp.zeros((8, TILE), f32)
    rr_static = over_tiles(first_static, zero)

    rr_members = zero
    waits, halos = halos, []
    for g in range(groups):
        for copy in waits[g]:
            copy.wait_recv()
        for cols in every:
            value = mul(t1_ref[small_of(g)], stacked(0, g, cols)) * c1_ref[small_of(g), 0:1]
            r0_ref[small_of(g), cols] = value
            x_ref[g, :, cols] = value.astype(bf16)
            rr_members = rr_members + squares(value, value)
        smooth(1, g)
        halos.append(send_halo(1, g))
    image(1, 0, r0s_ref, im0_ref, halos)

    def weigh(cols, acc):
        value = im0_ref[:, cols]
        weighted = p_ref[:, cols] * value
        gown_ref[:, cols] = weighted.astype(bf16)
        return acc + weighted * value

    q00 = over_tiles(weigh, zero)
    gall_ref[place(m)] = gown_ref[...]
    for o in range(1, members):
        push(
            gown_ref, gall_ref.at[place(m)], g_send.at[o - 1], g_recv.at[m], at_m(o), band
        )
    m_start(0, pack([total_of(rr_members + rr_static * (1.0 / members)), total_of(q00)]))
    for o in range(1, members):
        source = at_m(members - o)
        arrived(
            gown_ref, gall_ref.at[place(source)], g_send.at[o - 1], g_recv.at[source],
            at_m(o), band,
        )

    waits = []
    for g in range(groups):
        fold(g, lambda g, cols: gall_ref[g * each : (g + 1) * each, :, cols].astype(f32).reshape(
            large, TILE
        ))
        smooth(2, g)
        waits.append(send_halo(2, g))
    x_start(0, m_wait(0))

    def second_static(cols):
        field = gall_ref[:, :, cols].astype(f32).reshape(rows2, TILE).astype(bf16)
        r1s_ref[:, cols] = r0s_ref[:, cols] + static_share * (
            mul(krt_ref[0], field) + mul(krt_ref[1], field)
        )

    over_tiles(second_static)
    y_start(0, x_wait(0))
    tot_ref[0] = y_wait(0)
    rr0 = tot_ref[0, 0:1, 0:1]
    q00 = tot_ref[0, 1:2, 0:1]
    alpha0 = rr0 / (rr0 + q00)
    rr_members = zero
    cross_members = zero
    halos = []
    for g in range(groups):
        for copy in waits[g]:
            copy.wait_recv()
        for cols in every:
            first = r0_ref[small_of(g), cols]
            localized = mul(t1_ref[small_of(g)], stacked(2, g, cols)) * c1_ref[small_of(g), 0:1]
            value = first - alpha0 * (first + localized)
            r1_ref[small_of(g), cols] = value
            x_ref[g, :, cols] = value.astype(bf16)
            rr_members = rr_members + squares(value, value)
            cross_members = cross_members + squares(value, first)
        smooth(3, g)
        halos.append(send_halo(3, g))

    def second_static_residual(cols, acc):
        rr, cross = acc
        first = r0s_ref[:, cols]
        value = first - alpha0 * r1s_ref[:, cols]
        r1s_ref[:, cols] = value
        return rr + squares(value, value), cross + squares(value, first)

    rr_static, cross_static = over_tiles(second_static_residual, (zero, zero))
    image(3, 1, r1s_ref, im1_ref, halos)

    def second_sums(cols, acc):
        q11, q01 = acc
        value = im1_ref[:, cols]
        weighted = p_ref[:, cols] * value
        return q11 + weighted * value, q01 + weighted * im0_ref[:, cols]

    q11, q01 = over_tiles(second_sums, (zero, zero))
    share = 1.0 / members
    m_start(1, pack([
        total_of(rr_members + rr_static * share),
        total_of(cross_members + cross_static * share),
        total_of(q11),
        total_of(q01),
    ]))
    x_start(1, m_wait(1))
    y_start(1, x_wait(1))
    tot_ref[1] = y_wait(1)
    rr1 = tot_ref[1, 0:1, 0:1]
    cross = tot_ref[1, 1:2, 0:1]
    q11 = tot_ref[1, 2:3, 0:1]
    q01 = tot_ref[1, 3:4, 0:1]
    beta = rr1 / rr0
    length = rr1 + beta * (2.0 * cross + beta * rr0)
    curvature = length + q11 + beta * (2.0 * q01 + beta * q00)
    alpha1 = rr1 / curvature
    ahead = alpha0 + alpha1 * beta

    def finish(cols):
        outm_ref[:, cols] = ahead * r0_ref[:, cols] + alpha1 * r1_ref[:, cols]
        outs_ref[:, cols] = ahead * r0s_ref[:, cols] + alpha1 * r1s_ref[:, cols]
        inc_ref[:, cols] = ahead * im0_ref[:, cols] + alpha1 * im1_ref[:, cols]

    over_tiles(finish)
    for copy in sends:
        copy.wait_send()
    for sent, copy in later:
        pl.when(sent)(copy.wait_send)


def shards(ensemble, member_weight, member_of_slot, halfwidth, static_root, innovation, precision):
    f32, bf16 = jnp.float32, jnp.bfloat16
    _, slots, levels, rows, width = ensemble.shape
    members = lax.axis_size("member")
    bands = lax.axis_size("band")
    me = lax.axis_index("member")
    across = 4 if bands % 4 == 0 else 1
    up = bands // across
    groups = max(levels // 4, 1)
    each = levels // groups
    padded = -(-width // TILE) * TILE
    tiles = padded // TILE
    eight = slots * rows
    rows1, rows2 = levels * rows, levels * eight
    small, large = each * rows, each * eight

    def flat(field):
        field = field.reshape(slots, each, groups, rows, width)
        field = jnp.transpose(field, (2, 1, 0, 3, 4))
        field = jnp.pad(field, ((0, 0),) * 4 + ((0, padded - width),))
        return field.reshape(rows2, padded)

    precise = precision.astype(f32)
    ens = flat(ensemble[0].astype(f32))
    w0 = flat(innovation.astype(f32) * precise[None])
    own = lax.dynamic_slice_in_dim(precise, me, 1, 0)[0]
    own = jnp.pad(jnp.concatenate([own] * slots, axis=0), ((0, 0), (0, padded - width)))
    weights = jnp.asarray(window_weights(width, padded), bf16)

    vmem = pl.BlockSpec(memory_space=pltpu.VMEM)
    smem = pl.BlockSpec(memory_space=pltpu.SMEM)
    dma = pltpu.SemaphoreType.DMA
    outm, outs, inc = pl.pallas_call(
        functools.partial(kernel, members, bands, across, tiles, groups),
        out_shape=[
            jax.ShapeDtypeStruct((rows1, padded), f32),
            jax.ShapeDtypeStruct((rows1, padded), f32),
            jax.ShapeDtypeStruct((eight, padded), f32),
        ],
        in_specs=[smem] * 3 + [vmem] * 5,
        out_specs=[vmem] * 3,
        scratch_shapes=[
            pltpu.VMEM((rows1, 3 * small), bf16),
            pltpu.VMEM((rows2, 3 * small), bf16),
            pltpu.VMEM((rows1, 128), f32),
            pltpu.VMEM((rows2, 128), f32),
            pltpu.VMEM((small, large), bf16),
            pltpu.VMEM((2, rows1, rows2), bf16),
            pltpu.VMEM((2, eight, rows1), bf16),
            pltpu.VMEM((groups, small, padded), bf16),
            pltpu.VMEM((4, groups, small, padded), bf16),
            pltpu.VMEM((4, groups, small, padded), bf16),
            pltpu.VMEM((4, groups, small, padded), bf16),
            pltpu.VMEM((2, levels, eight, padded), bf16),
            pltpu.VMEM((2, members, eight, padded), bf16),
            pltpu.VMEM((eight, padded), bf16),
            pltpu.VMEM((levels, eight, padded), bf16),
            pltpu.VMEM((rows1, padded), f32),
            pltpu.VMEM((rows1, padded), f32),
            pltpu.VMEM((rows1, padded), f32),
            pltpu.VMEM((rows1, padded), f32),
            pltpu.VMEM((eight, padded), f32),
            pltpu.VMEM((eight, padded), f32),
            pltpu.VMEM((2, 3, 8, 128), f32),
            pltpu.VMEM((2, 8, 128), f32),
            pltpu.VMEM((2, members, 8, 128), f32),
            pltpu.VMEM((2, across, 8, 128), f32),
            pltpu.VMEM((2, up, 8, 128), f32),
            dma((4, groups, 2)),
            dma((4, groups, 2)),
            dma((2, members)),
            dma((2, members)),
            dma((members,)),
            dma((members,)),
            dma((2, members - 1)),
            dma((2, members - 1)),
            dma((2, max(across - 1, 1))),
            dma((2, max(across - 1, 1))),
            dma((2, max(up - 1, 1))),
            dma((2, max(up - 1, 1))),
        ],
        compiler_params=pltpu.CompilerParams(collective_id=0, has_side_effects=True),
    )(member_weight, member_of_slot, halfwidth, ens, w0, own, static_root, weights)

    def unflat(field):
        field = field[:, :width].reshape(groups, each, rows, width)
        return jnp.transpose(field, (1, 0, 2, 3)).reshape(levels, rows, width)

    increment = inc[:, :width].reshape(slots, 1, rows, width)
    return unflat(outm)[None], unflat(outs), increment


def solution(mesh):
    return jax.shard_map(
        shards,
        mesh=mesh,
        in_specs=(
            P("member", None, None, "band", None),
            P(),
            P("member"),
            P(),
            P(),
            P(None, None, "band", None),
            P(None, "band", None),
        ),
        out_specs=(
            P("member", None, "band", None),
            P(None, "band", None),
            P(None, "member", "band", None),
        ),
        check_vma=False,
    )
```

```python
import functools
import math

import jax
import jax.numpy as jnp
import numpy as np
from jax import lax
from jax.experimental import pallas as pl
from jax.experimental.pallas import tpu as pltpu
from jax.sharding import PartitionSpec as P

HMAX = 4
LREACH = 18
TILE = 256
EDGE = 128

ensemble_share = 0.8
static_share = 0.6
length_scale = 6.0
MESH = pl.DeviceIdType.MESH


def window_weights(width, padded):
    tiles = padded // TILE
    kinds = []
    for tile in (0, 1, tiles - 1):
        start = tile * TILE
        rows = np.arange(start - EDGE, start + TILE + EDGE)
        if tile == 0:
            rows[:EDGE] = np.arange(padded - EDGE, padded)
        if tile == tiles - 1:
            rows[-EDGE:] = np.arange(EDGE)
        cols = np.arange(start, start + TILE)
        apart = np.abs(rows[:, None] - cols[None, :])
        apart = np.minimum(apart, width - apart)
        near = (apart <= LREACH) & (rows[:, None] < width) & (cols[None, :] < width)
        distance = apart.astype(np.float32)
        values = np.exp(-0.5 * (distance / np.float32(length_scale)) ** 2) / np.float32(
            length_scale * math.sqrt(2.0 * math.pi)
        )
        kinds.append(np.where(near, values, 0.0).astype(np.float32))
    return np.stack(kinds)


def mul(a, b):
    return jnp.dot(a, b, preferred_element_type=jnp.float32)


def mul_wide(weights, field):
    high = field.astype(jnp.bfloat16)
    low = (field - high.astype(jnp.float32)).astype(jnp.bfloat16)
    return mul(weights[0], high) + mul(weights[0], low) + mul(weights[1], high)


def kernel(
    members, bands, across, tiles, groups,
    weight_ref, slot_ref, half_ref,
    ens_ref, w0_ref, p_ref, root_ref, wk_ref,
    outm_ref, outs_ref, inc_ref,
    t1_ref, t2_ref, c1_ref, c2_ref, sel_ref, krt_ref, krm_ref,
    x_ref, s_ref, hp_ref, hn_ref, part_ref, pair_ref, sum_ref, rs_ref, gown_ref, gall_ref,
    r0_ref, r1_ref, r0s_ref, r1s_ref, im0_ref, im1_ref,
    vec_ref, tot_ref, allm_ref, allx_ref, ally_ref,
    h_send, h_recv, pair_send, pair_recv, rs_send, rs_recv, g_send, g_recv, m_send, m_recv, x_send, x_recv, y_send, y_recv,
):
    f32, bf16 = jnp.float32, jnp.bfloat16
    m = lax.axis_index("member")
    band = lax.axis_index("band")
    up = bands // across
    by = band // across
    bx = lax.rem(band, across)
    levels, eight = gall_ref.shape[0], gall_ref.shape[1]
    rows = eight // 2
    rows1, rows2 = levels * rows, levels * eight
    each = levels // groups
    small, large = each * rows, each * eight
    chips = members // 2
    core = lax.rem(m, 2)
    chip = m // 2
    partner = m + 1 - 2 * core
    my_group = lax.rem(m, groups)
    my_place = m // groups

    def at_m(o):
        return lax.rem(m + o, members)

    def at_band(o):
        return lax.rem(band + o, bands)

    def x_peer(o):
        return lax.rem(bx + o, across)

    def y_peer(o):
        return lax.rem(by + o, up)

    def place(level):
        return lax.rem(level, groups) * each + level // groups

    barrier = pltpu.get_barrier_semaphore()
    greeted = 0
    for o in range(1, members):
        pl.semaphore_signal(
            barrier, inc=1, device_id=(at_m(o), band), device_id_type=MESH
        )
        greeted += 1
    others = [at_band(1), at_band(bands - 1)]
    others += [by * across + x_peer(o) for o in range(1, across)]
    others += [y_peer(o) * across + bx for o in range(1, up)]
    for other in others:
        pl.semaphore_signal(barrier, inc=1, device_id=(m, other), device_id_type=MESH)
        greeted += 1

    def iota(shape, axis):
        return lax.broadcasted_iota(jnp.int32, shape, axis)

    def over(index, size):
        return lax.shift_right_logical(index, size.bit_length() - 1)

    def level_of(index, height):
        inside = index & (each * height - 1)
        return over(inside, height) * groups + over(index, each * height)

    def span_of(level):
        span = jnp.zeros(level.shape, jnp.int32)
        for at in range(levels):
            span = jnp.where(level == at, half_ref[at] + 1, span)
        return span

    low_side = jnp.where(band > 0, 1, 0)
    high_side = jnp.where(band < bands - 1, 1, 0)
    scaled = jnp.float32(0.0)
    for at in range(members):
        scaled = scaled + jnp.where(slot_ref[0] == at, weight_ref[at], 0.0)

    def taper(height, out, factors, extra):
        shape = (levels * height, 3 * small)
        line, col = iota(shape, 0), iota(shape, 1)
        side = jnp.where(col >= small, 1, 0) + jnp.where(col >= 2 * small, 1, 0)
        within = col - side * small
        apart = jnp.abs((within & (rows - 1)) + (side - 1) * rows - (line & (rows - 1)))
        same = over(within, rows) == over(line & (each * height - 1), height)
        seen = jnp.where(side == 0, low_side, jnp.where(side == 2, high_side, 1)) == 1
        span = span_of(level_of(line, height))
        values = jnp.where(same & seen, jnp.maximum(span - apart, 0), 0)
        out[...] = values.astype(f32).astype(bf16)
        spans = span_of(level_of(iota(factors.shape, 0), height)).astype(f32)
        factors[...] = extra / (spans * spans)

    taper(rows, t1_ref, c1_ref, ensemble_share)
    taper(eight, t2_ref, c2_ref, ensemble_share * scaled)

    def ones(condition):
        return jnp.where(condition, 1.0, 0.0).astype(f32)

    line, col = iota((small, large), 0), iota((small, large), 1)
    picked = over(line, rows) * eight + (line & (rows - 1))
    sel_ref[...] = ones(col == picked).astype(bf16)
    shape = (rows1, levels)
    place1 = ones(level_of(iota(shape, 0), rows) == iota(shape, 1)).astype(bf16)
    shape = (levels, rows2)
    level2 = ones(level_of(iota(shape, 1), eight) == iota(shape, 0)).astype(bf16)
    shape = (levels, rows1)
    level1 = ones(level_of(iota(shape, 1), rows) == iota(shape, 0)).astype(bf16)
    shape = (eight, levels)
    mine = ones(iota(shape, 1) == m).astype(bf16)
    shape = (rows1, rows2)
    match = ones((iota(shape, 0) & (rows - 1)) == (iota(shape, 1) & (rows - 1)))
    shape = (eight, rows1)
    match_row = ones((iota(shape, 0) & (rows - 1)) == (iota(shape, 1) & (rows - 1)))
    root = root_ref[...]
    root_high = root.astype(bf16)
    root_low = (root - root_high.astype(f32)).astype(bf16)
    for at, piece in enumerate((root_high, root_low)):
        spread = lax.dot_general(
            place1, piece, (((1,), (1,)), ((), ())), preferred_element_type=f32
        )
        krt_ref[at] = (mul(spread.astype(bf16), level2) * match).astype(bf16)
        spread = mul(mine, piece)
        krm_ref[at] = (mul(spread.astype(bf16), level1) * match_row).astype(bf16)

    sends = []

    def push(src, dst, send, recv, member, other):
        copy = pltpu.make_async_remote_copy(
            src_ref=src, dst_ref=dst, send_sem=send, recv_sem=recv,
            device_id=(member, other), device_id_type=MESH,
        )
        copy.start()
        sends.append(copy)
        return copy

    def arrived(like, dst, send, recv, member, other):
        pltpu.make_async_remote_copy(
            src_ref=like, dst_ref=dst, send_sem=send, recv_sem=recv,
            device_id=(member, other), device_id_type=MESH,
        ).wait_recv()

    def columns(i):
        return pl.ds(pl.multiple_of(i * TILE, TILE), TILE)

    def over_tiles(body, init=None):
        if init is None:
            def step(i, carry):
                body(columns(i))
                return carry
            lax.fori_loop(0, tiles, step, 0)
            return None
        return lax.fori_loop(0, tiles, lambda i, carry: body(columns(i), carry), init)

    every = [slice(i * TILE, (i + 1) * TILE) for i in range(tiles)]
    last = tiles * TILE

    def smooth(phase, g):
        for i, cols in enumerate(every):
            start, stop = i * TILE - EDGE, (i + 1) * TILE + EDGE
            if i == 0:
                window = jnp.concatenate([x_ref[g, :, last - EDGE :], x_ref[g, :, :stop]], axis=1)
            elif i == tiles - 1:
                window = jnp.concatenate([x_ref[g, :, start:], x_ref[g, :, :EDGE]], axis=1)
            else:
                window = x_ref[g, :, start:stop]
            kind = 0 if i == 0 else 2 if i == tiles - 1 else 1
            s_ref[phase, g, :, cols] = mul(window, wk_ref[kind]).astype(bf16)

    def send_halo(phase, g):
        return (
            push(
                s_ref.at[phase, g], hp_ref.at[phase, g], h_send.at[phase, g, 0],
                h_recv.at[phase, g, 0], m, at_band(1),
            ),
            push(
                s_ref.at[phase, g], hn_ref.at[phase, g], h_send.at[phase, g, 1],
                h_recv.at[phase, g, 1], m, at_band(bands - 1),
            ),
        )

    def small_of(g):
        return slice(g * small, (g + 1) * small)

    def large_of(g):
        return slice(g * large, (g + 1) * large)

    def stacked(phase, g, cols):
        return jnp.concatenate(
            [hp_ref[phase, g, :, cols], s_ref[phase, g, :, cols], hn_ref[phase, g, :, cols]],
            axis=0,
        )

    def fold(g, field):
        for cols in every:
            products = (ens_ref[large_of(g), cols] * field(g, cols)).reshape(each, eight, TILE)
            both = (products + pltpu.roll(products, rows, 1)) * scaled
            both = both.reshape(large, TILE).astype(bf16)
            x_ref[g, :, cols] = mul(sel_ref[...], both).astype(bf16)

    def squares(a, b):
        product = a * b
        return jnp.sum(product.reshape(product.shape[0] // 8, 8, TILE), axis=0)

    def pair_copy(stage, g):
        return pltpu.make_async_remote_copy(
            src_ref=part_ref.at[stage, g * each : (g + 1) * each],
            dst_ref=pair_ref.at[stage, g],
            send_sem=pair_send.at[stage, g], recv_sem=pair_recv.at[stage, g],
            device_id=(partner, band), device_id_type=MESH,
        )

    def sum_copy(stage, g, o):
        there = lax.rem(my_place + o, each)
        return pltpu.make_async_remote_copy(
            src_ref=sum_ref.at[stage, g * each + there], dst_ref=rs_ref.at[stage, chip],
            send_sem=rs_send.at[stage, g * each + o], recv_sem=rs_recv.at[stage, chip],
            device_id=(there * groups + g, band), device_id_type=MESH,
        )

    def forward(stage, g):
        @pl.when(core == g % 2)
        def _():
            pair_copy(stage, g).wait_recv()
            span = slice(g * each, (g + 1) * each)
            for cols in every:
                sum_ref[stage, span, :, cols] = (
                    part_ref[stage, span, :, cols].astype(f32)
                    + pair_ref[stage, g, :, :, cols].astype(f32)
                ).astype(bf16)
            for o in range(1, each):
                sum_copy(stage, g, o).start()
            pl.when(my_group != g)(sum_copy(stage, g, 0).start)

            @pl.when(my_group == g)
            def _():
                rs_ref[stage, chip] = sum_ref[stage, place(m)]

    def settle(stage, g):
        pl.when(core != g % 2)(pair_copy(stage, g).wait_send)

        @pl.when(core == g % 2)
        def _():
            for o in range(1, each):
                sum_copy(stage, g, o).wait_send()
            pl.when(my_group != g)(sum_copy(stage, g, 0).wait_send)

    def image(phase, stage, static_ref, out, halos):
        def static(cols):
            out[:, cols] = static_share * mul_wide(krm_ref, static_ref[:, cols])

        over_tiles(static)
        for g in range(groups):
            for copy in halos[g]:
                copy.wait_recv()
            for cols in every:
                localized = mul(t2_ref[large_of(g)], stacked(phase, g, cols))
                products = localized * c2_ref[large_of(g), 0:1] * ens_ref[large_of(g), cols]
                part_ref[stage, g * each : (g + 1) * each, :, cols] = products.reshape(
                    each, eight, TILE
                ).astype(bf16)
            if g > 0:
                forward(stage, g - 1)
            pl.when(core != g % 2)(pair_copy(stage, g).start)
        forward(stage, groups - 1)
        for o in range(1, chips):
            source = lax.rem(chip + chips - o, chips)
            arrived(
                sum_ref.at[stage, 0], rs_ref.at[stage, source], rs_send.at[stage, 0],
                rs_recv.at[stage, source], at_m(2 * o), band,
            )

        def collect(cols):
            out[:, cols] = out[:, cols] + jnp.sum(rs_ref[stage, :, :, cols].astype(f32), axis=0)

        over_tiles(collect)

    def total_of(acc):
        return jnp.sum(jnp.sum(acc, axis=1, keepdims=True), axis=0, keepdims=True)

    def pack(values):
        line = iota((8, 128), 0)
        packed = jnp.zeros((8, 128), f32)
        for at, value in enumerate(values):
            packed = jnp.where(line == at, value, packed)
        return packed

    def gather_start(k, stage, value, table, count, own, peer, send, recv):
        vec_ref[k, stage] = value
        table[k, own] = value
        for o in range(1, count):
            member, other = peer(o)
            push(
                vec_ref.at[k, stage], table.at[k, own], send.at[k, o - 1], recv.at[k, o - 1],
                member, other,
            )

    def gather_wait(k, stage, table, count, source, peer, send, recv):
        for o in range(1, count):
            member, other = peer(o)
            arrived(
                vec_ref.at[k, stage], table.at[k, source(o)], send.at[k, o - 1],
                recv.at[k, o - 1], member, other,
            )
        return jnp.sum(table[k], axis=0)

    def m_to(o):
        return at_m(o), band

    def x_to(o):
        return m, by * across + x_peer(o)

    def y_to(o):
        return m, y_peer(o) * across + bx

    def m_start(k, value):
        gather_start(k, 0, value, allm_ref, members, m, m_to, m_send, m_recv)

    def m_wait(k):
        return gather_wait(k, 0, allm_ref, members, lambda o: at_m(members - o), m_to, m_send, m_recv)

    def x_start(k, value):
        gather_start(k, 1, value, allx_ref, across, bx, x_to, x_send, x_recv)

    def x_wait(k):
        return gather_wait(k, 1, allx_ref, across, lambda o: x_peer(across - o), x_to, x_send, x_recv)

    def y_start(k, value):
        gather_start(k, 2, value, ally_ref, up, by, y_to, y_send, y_recv)

    def y_wait(k):
        return gather_wait(k, 2, ally_ref, up, lambda o: y_peer(up - o), y_to, y_send, y_recv)

    halos = []
    for g in range(groups):
        fold(g, lambda g, cols: w0_ref[large_of(g), cols])
        smooth(0, g)
        if g == 0:
            pl.semaphore_wait(barrier, greeted)
        halos.append(send_halo(0, g))

    def first_static(cols, acc):
        value = static_share * mul_wide(krt_ref, w0_ref[:, cols])
        r0s_ref[:, cols] = value
        return acc + squares(value, value)

    zero = jnp.zeros((8, TILE), f32)
    rr_static = over_tiles(first_static, zero)

    rr_members = zero
    waits, halos = halos, []
    for g in range(groups):
        for copy in waits[g]:
            copy.wait_recv()
        for cols in every:
            value = mul(t1_ref[small_of(g)], stacked(0, g, cols)) * c1_ref[small_of(g), 0:1]
            r0_ref[small_of(g), cols] = value
            x_ref[g, :, cols] = value.astype(bf16)
            rr_members = rr_members + squares(value, value)
        smooth(1, g)
        halos.append(send_halo(1, g))
    image(1, 0, r0s_ref, im0_ref, halos)

    def weigh(cols, acc):
        value = im0_ref[:, cols]
        weighted = p_ref[:, cols] * value
        gown_ref[:, cols] = weighted.astype(bf16)
        return acc + weighted * value

    q00 = over_tiles(weigh, zero)
    gall_ref[place(m)] = gown_ref[...]
    m_start(0, pack([total_of(rr_members + rr_static * (1.0 / members)), total_of(q00)]))
    order = sorted(range(1, chips), key=lambda o: min(o, chips - o))
    for o in order[::-1]:
        push(gown_ref, gall_ref.at[place(m)], g_send.at[o], g_recv.at[m], at_m(2 * o), band)
    push(gown_ref, gall_ref.at[place(m)], g_send.at[0], g_recv.at[m], partner, band)
    x_start(0, m_wait(0))
    for o in order:
        source = at_m(members - 2 * o)
        spot = gall_ref.at[place(source)]
        arrived(gown_ref, spot, g_send.at[o], g_recv.at[source], at_m(2 * o), band)
        push(spot, spot, g_send.at[chips + o], g_recv.at[source], partner, band)
    y_start(0, x_wait(0))
    for o in [0] + order:
        source = lax.rem(partner + members - 2 * o, members)
        spot = gall_ref.at[place(source)]
        arrived(gown_ref, spot, g_send.at[0], g_recv.at[source], partner, band)

    waits = []
    for g in range(groups):
        fold(g, lambda g, cols: gall_ref[g * each : (g + 1) * each, :, cols].astype(f32).reshape(
            large, TILE
        ))
        smooth(2, g)
        waits.append(send_halo(2, g))

    def second_static(cols):
        field = gall_ref[:, :, cols].astype(f32).reshape(rows2, TILE).astype(bf16)
        r1s_ref[:, cols] = r0s_ref[:, cols] + static_share * (
            mul(krt_ref[0], field) + mul(krt_ref[1], field)
        )

    over_tiles(second_static)
    tot_ref[0] = y_wait(0)
    rr0 = tot_ref[0, 0:1, 0:1]
    q00 = tot_ref[0, 1:2, 0:1]
    alpha0 = rr0 / (rr0 + q00)
    rr_members = zero
    cross_members = zero
    halos = []
    for g in range(groups):
        for copy in waits[g]:
            copy.wait_recv()
        for cols in every:
            first = r0_ref[small_of(g), cols]
            localized = mul(t1_ref[small_of(g)], stacked(2, g, cols)) * c1_ref[small_of(g), 0:1]
            value = first - alpha0 * (first + localized)
            r1_ref[small_of(g), cols] = value
            x_ref[g, :, cols] = value.astype(bf16)
            rr_members = rr_members + squares(value, value)
            cross_members = cross_members + squares(value, first)
        smooth(3, g)
        halos.append(send_halo(3, g))

    def second_static_residual(cols, acc):
        rr, cross = acc
        first = r0s_ref[:, cols]
        value = first - alpha0 * r1s_ref[:, cols]
        r1s_ref[:, cols] = value
        return rr + squares(value, value), cross + squares(value, first)

    rr_static, cross_static = over_tiles(second_static_residual, (zero, zero))
    image(3, 1, r1s_ref, im1_ref, halos)

    def second_sums(cols, acc):
        q11, q01 = acc
        value = im1_ref[:, cols]
        weighted = p_ref[:, cols] * value
        return q11 + weighted * value, q01 + weighted * im0_ref[:, cols]

    q11, q01 = over_tiles(second_sums, (zero, zero))
    share = 1.0 / members
    m_start(1, pack([
        total_of(rr_members + rr_static * share),
        total_of(cross_members + cross_static * share),
        total_of(q11),
        total_of(q01),
    ]))
    x_start(1, m_wait(1))
    y_start(1, x_wait(1))
    tot_ref[1] = y_wait(1)
    rr1 = tot_ref[1, 0:1, 0:1]
    cross = tot_ref[1, 1:2, 0:1]
    q11 = tot_ref[1, 2:3, 0:1]
    q01 = tot_ref[1, 3:4, 0:1]
    beta = rr1 / rr0
    length = rr1 + beta * (2.0 * cross + beta * rr0)
    curvature = length + q11 + beta * (2.0 * q01 + beta * q00)
    alpha1 = rr1 / curvature
    ahead = alpha0 + alpha1 * beta

    def finish(cols):
        outm_ref[:, cols] = ahead * r0_ref[:, cols] + alpha1 * r1_ref[:, cols]
        outs_ref[:, cols] = ahead * r0s_ref[:, cols] + alpha1 * r1s_ref[:, cols]
        inc_ref[:, cols] = ahead * im0_ref[:, cols] + alpha1 * im1_ref[:, cols]

    over_tiles(finish)
    for copy in sends:
        copy.wait_send()
    for stage in range(2):
        for g in range(groups):
            settle(stage, g)


def shards(ensemble, member_weight, member_of_slot, halfwidth, static_root, innovation, precision):
    f32, bf16 = jnp.float32, jnp.bfloat16
    _, slots, levels, rows, width = ensemble.shape
    members = lax.axis_size("member")
    bands = lax.axis_size("band")
    me = lax.axis_index("member")
    across = 4 if bands % 4 == 0 else 1
    up = bands // across
    groups = max(levels // 4, 1)
    each = levels // groups
    padded = -(-width // TILE) * TILE
    tiles = padded // TILE
    eight = slots * rows
    rows1, rows2 = levels * rows, levels * eight
    small, large = each * rows, each * eight

    def flat(field):
        field = field.reshape(slots, each, groups, rows, width)
        field = jnp.transpose(field, (2, 1, 0, 3, 4))
        field = jnp.pad(field, ((0, 0),) * 4 + ((0, padded - width),))
        return field.reshape(rows2, padded)

    precise = precision.astype(f32)
    ens = flat(ensemble[0].astype(f32))
    w0 = flat(innovation.astype(f32) * precise[None])
    own = lax.dynamic_slice_in_dim(precise, me, 1, 0)[0]
    own = jnp.pad(jnp.concatenate([own] * slots, axis=0), ((0, 0), (0, padded - width)))
    weights = jnp.asarray(window_weights(width, padded), bf16)

    vmem = pl.BlockSpec(memory_space=pltpu.VMEM)
    smem = pl.BlockSpec(memory_space=pltpu.SMEM)
    dma = pltpu.SemaphoreType.DMA
    outm, outs, inc = pl.pallas_call(
        functools.partial(kernel, members, bands, across, tiles, groups),
        out_shape=[
            jax.ShapeDtypeStruct((rows1, padded), f32),
            jax.ShapeDtypeStruct((rows1, padded), f32),
            jax.ShapeDtypeStruct((eight, padded), f32),
        ],
        in_specs=[smem] * 3 + [vmem] * 5,
        out_specs=[vmem] * 3,
        scratch_shapes=[
            pltpu.VMEM((rows1, 3 * small), bf16),
            pltpu.VMEM((rows2, 3 * small), bf16),
            pltpu.VMEM((rows1, 128), f32),
            pltpu.VMEM((rows2, 128), f32),
            pltpu.VMEM((small, large), bf16),
            pltpu.VMEM((2, rows1, rows2), bf16),
            pltpu.VMEM((2, eight, rows1), bf16),
            pltpu.VMEM((groups, small, padded), bf16),
            pltpu.VMEM((4, groups, small, padded), bf16),
            pltpu.VMEM((4, groups, small, padded), bf16),
            pltpu.VMEM((4, groups, small, padded), bf16),
            pltpu.VMEM((2, levels, eight, padded), bf16),
            pltpu.VMEM((2, groups, each, eight, padded), bf16),
            pltpu.VMEM((2, levels, eight, padded), bf16),
            pltpu.VMEM((2, members // 2, eight, padded), bf16),
            pltpu.VMEM((eight, padded), bf16),
            pltpu.VMEM((levels, eight, padded), bf16),
            pltpu.VMEM((rows1, padded), f32),
            pltpu.VMEM((rows1, padded), f32),
            pltpu.VMEM((rows1, padded), f32),
            pltpu.VMEM((rows1, padded), f32),
            pltpu.VMEM((eight, padded), f32),
            pltpu.VMEM((eight, padded), f32),
            pltpu.VMEM((2, 3, 8, 128), f32),
            pltpu.VMEM((2, 8, 128), f32),
            pltpu.VMEM((2, members, 8, 128), f32),
            pltpu.VMEM((2, across, 8, 128), f32),
            pltpu.VMEM((2, up, 8, 128), f32),
            dma((4, groups, 2)),
            dma((4, groups, 2)),
            dma((2, groups)),
            dma((2, groups)),
            dma((2, members)),
            dma((2, members // 2)),
            dma((members,)),
            dma((members,)),
            dma((2, members - 1)),
            dma((2, members - 1)),
            dma((2, max(across - 1, 1))),
            dma((2, max(across - 1, 1))),
            dma((2, max(up - 1, 1))),
            dma((2, max(up - 1, 1))),
        ],
        compiler_params=pltpu.CompilerParams(collective_id=0, has_side_effects=True),
    )(member_weight, member_of_slot, halfwidth, ens, w0, own, static_root, weights)

    def unflat(field):
        field = field[:, :width].reshape(groups, each, rows, width)
        return jnp.transpose(field, (1, 0, 2, 3)).reshape(levels, rows, width)

    increment = inc[:, :width].reshape(slots, 1, rows, width)
    return unflat(outm)[None], unflat(outs), increment


def solution(mesh):
    return jax.shard_map(
        shards,
        mesh=mesh,
        in_specs=(
            P("member", None, None, "band", None),
            P(),
            P("member"),
            P(),
            P(),
            P(None, None, "band", None),
            P(None, "band", None),
        ),
        out_specs=(
            P("member", None, "band", None),
            P(None, "band", None),
            P(None, "member", "band", None),
        ),
        check_vma=False,
    )
```

```python
import functools
import math

import jax
import jax.numpy as jnp
import numpy as np
from jax import lax
from jax.experimental import pallas as pl
from jax.experimental.pallas import tpu as pltpu
from jax.sharding import PartitionSpec as P

HMAX = 4
LREACH = 18
TILE = 256
EDGE = 128

ensemble_share = 0.8
static_share = 0.6
length_scale = 6.0
MESH = pl.DeviceIdType.MESH


def window_weights(width, padded):
    tiles = padded // TILE
    kinds = []
    for tile in (0, 1, tiles - 1):
        start = tile * TILE
        rows = np.arange(start - EDGE, start + TILE + EDGE)
        if tile == 0:
            rows[:EDGE] = np.arange(padded - EDGE, padded)
        if tile == tiles - 1:
            rows[-EDGE:] = np.arange(EDGE)
        cols = np.arange(start, start + TILE)
        apart = np.abs(rows[:, None] - cols[None, :])
        apart = np.minimum(apart, width - apart)
        near = (apart <= LREACH) & (rows[:, None] < width) & (cols[None, :] < width)
        distance = apart.astype(np.float32)
        values = np.exp(-0.5 * (distance / np.float32(length_scale)) ** 2) / np.float32(
            length_scale * math.sqrt(2.0 * math.pi)
        )
        kinds.append(np.where(near, values, 0.0).astype(np.float32))
    return np.stack(kinds)


def mul(a, b):
    return jnp.dot(a, b, preferred_element_type=jnp.float32)


def mul_wide(weights, field):
    high = field.astype(jnp.bfloat16)
    low = (field - high.astype(jnp.float32)).astype(jnp.bfloat16)
    return mul(weights[0], high) + mul(weights[0], low) + mul(weights[1], high)


def kernel(
    members, bands, across, tiles, groups,
    weight_ref, slot_ref, half_ref,
    raw_ref, innov_ref, prec_ref, root_ref, wk_ref,
    outm_ref, outs_ref, inc_ref,
    ens_ref, w0_ref, p_ref,
    t1_ref, t2_ref, c1_ref, c2_ref, sel_ref, krt_ref, krm_ref,
    x_ref, s_ref, hp_ref, hn_ref, part_ref, pair_ref, sum_ref, rs_ref, gown_ref, gall_ref,
    r0_ref, r1_ref, r0s_ref, r1s_ref, im0_ref, im1_ref,
    vec_ref, tot_ref, allm_ref, allx_ref, ally_ref,
    h_send, h_recv, pair_send, pair_recv, rs_send, rs_recv, g_send, g_recv, m_send, m_recv, x_send, x_recv, y_send, y_recv,
):
    f32, bf16 = jnp.float32, jnp.bfloat16
    m = lax.axis_index("member")
    band = lax.axis_index("band")
    up = bands // across
    by = band // across
    bx = lax.rem(band, across)
    levels, eight = gall_ref.shape[0], gall_ref.shape[1]
    rows = eight // 2
    rows1, rows2 = levels * rows, levels * eight
    each = levels // groups
    small, large = each * rows, each * eight
    chips = members // 2
    core = lax.rem(m, 2)
    chip = m // 2
    partner = m + 1 - 2 * core
    my_group = lax.rem(m, groups)
    my_place = m // groups

    def at_m(o):
        return lax.rem(m + o, members)

    def at_band(o):
        return lax.rem(band + o, bands)

    def x_peer(o):
        return lax.rem(bx + o, across)

    def y_peer(o):
        return lax.rem(by + o, up)

    def place(level):
        return lax.rem(level, groups) * each + level // groups

    barrier = pltpu.get_barrier_semaphore()
    greeted = 0
    for o in range(1, members):
        pl.semaphore_signal(
            barrier, inc=1, device_id=(at_m(o), band), device_id_type=MESH
        )
        greeted += 1
    others = [at_band(1), at_band(bands - 1)]
    others += [by * across + x_peer(o) for o in range(1, across)]
    others += [y_peer(o) * across + bx for o in range(1, up)]
    for other in others:
        pl.semaphore_signal(barrier, inc=1, device_id=(m, other), device_id_type=MESH)
        greeted += 1

    def iota(shape, axis):
        return lax.broadcasted_iota(jnp.int32, shape, axis)

    def over(index, size):
        return lax.shift_right_logical(index, size.bit_length() - 1)

    def level_of(index, height):
        inside = index & (each * height - 1)
        return over(inside, height) * groups + over(index, each * height)

    def span_of(level):
        span = jnp.zeros(level.shape, jnp.int32)
        for at in range(levels):
            span = jnp.where(level == at, half_ref[at] + 1, span)
        return span

    low_side = jnp.where(band > 0, 1, 0)
    high_side = jnp.where(band < bands - 1, 1, 0)
    scaled = jnp.float32(0.0)
    for at in range(members):
        scaled = scaled + jnp.where(slot_ref[0] == at, weight_ref[at], 0.0)

    def taper(height, out, factors, extra):
        shape = (levels * height, 3 * small)
        line, col = iota(shape, 0), iota(shape, 1)
        side = jnp.where(col >= small, 1, 0) + jnp.where(col >= 2 * small, 1, 0)
        within = col - side * small
        apart = jnp.abs((within & (rows - 1)) + (side - 1) * rows - (line & (rows - 1)))
        same = over(within, rows) == over(line & (each * height - 1), height)
        seen = jnp.where(side == 0, low_side, jnp.where(side == 2, high_side, 1)) == 1
        span = span_of(level_of(line, height))
        values = jnp.where(same & seen, jnp.maximum(span - apart, 0), 0)
        out[...] = values.astype(f32).astype(bf16)
        spans = span_of(level_of(iota(factors.shape, 0), height)).astype(f32)
        factors[...] = extra / (spans * spans)

    taper(rows, t1_ref, c1_ref, ensemble_share)
    taper(eight, t2_ref, c2_ref, ensemble_share * scaled)

    def ones(condition):
        return jnp.where(condition, 1.0, 0.0).astype(f32)

    line, col = iota((small, large), 0), iota((small, large), 1)
    picked = over(line, rows) * eight + (line & (rows - 1))
    sel_ref[...] = ones(col == picked).astype(bf16)
    shape = (rows1, levels)
    place1 = ones(level_of(iota(shape, 0), rows) == iota(shape, 1)).astype(bf16)
    shape = (levels, rows2)
    level2 = ones(level_of(iota(shape, 1), eight) == iota(shape, 0)).astype(bf16)
    shape = (levels, rows1)
    level1 = ones(level_of(iota(shape, 1), rows) == iota(shape, 0)).astype(bf16)
    shape = (eight, levels)
    mine = ones(iota(shape, 1) == m).astype(bf16)
    shape = (rows1, rows2)
    match = ones((iota(shape, 0) & (rows - 1)) == (iota(shape, 1) & (rows - 1)))
    shape = (eight, rows1)
    match_row = ones((iota(shape, 0) & (rows - 1)) == (iota(shape, 1) & (rows - 1)))
    root = root_ref[...]
    root_high = root.astype(bf16)
    root_low = (root - root_high.astype(f32)).astype(bf16)
    for at, piece in enumerate((root_high, root_low)):
        spread = lax.dot_general(
            place1, piece, (((1,), (1,)), ((), ())), preferred_element_type=f32
        )
        krt_ref[at] = (mul(spread.astype(bf16), level2) * match).astype(bf16)
        spread = mul(mine, piece)
        krm_ref[at] = (mul(spread.astype(bf16), level1) * match_row).astype(bf16)

    width = prec_ref.shape[2]
    for target in (ens_ref, w0_ref, p_ref):
        target[:, width - width % 128 :] = jnp.zeros(
            (target.shape[0], target.shape[1] - width + width % 128), f32
        )

    def load(g):
        for j in range(each):
            level = j * groups + g
            lines = slice((g * each + j) * eight, (g * each + j + 1) * eight)
            precise = prec_ref[level].astype(f32)
            ens_ref[lines, :width] = jnp.concatenate(
                [raw_ref[0, t, level].astype(f32) for t in range(2)], axis=0
            )
            w0_ref[lines, :width] = jnp.concatenate(
                [innov_ref[t, level].astype(f32) * precise for t in range(2)], axis=0
            )

    sends = []

    def push(src, dst, send, recv, member, other):
        copy = pltpu.make_async_remote_copy(
            src_ref=src, dst_ref=dst, send_sem=send, recv_sem=recv,
            device_id=(member, other), device_id_type=MESH,
        )
        copy.start()
        sends.append(copy)
        return copy

    def arrived(like, dst, send, recv, member, other):
        pltpu.make_async_remote_copy(
            src_ref=like, dst_ref=dst, send_sem=send, recv_sem=recv,
            device_id=(member, other), device_id_type=MESH,
        ).wait_recv()

    def columns(i):
        return pl.ds(pl.multiple_of(i * TILE, TILE), TILE)

    def over_tiles(body, init=None):
        if init is None:
            def step(i, carry):
                body(columns(i))
                return carry
            lax.fori_loop(0, tiles, step, 0)
            return None
        return lax.fori_loop(0, tiles, lambda i, carry: body(columns(i), carry), init)

    every = [slice(i * TILE, (i + 1) * TILE) for i in range(tiles)]
    last = tiles * TILE

    def smooth(phase, g):
        for i, cols in enumerate(every):
            start, stop = i * TILE - EDGE, (i + 1) * TILE + EDGE
            if i == 0:
                window = jnp.concatenate([x_ref[g, :, last - EDGE :], x_ref[g, :, :stop]], axis=1)
            elif i == tiles - 1:
                window = jnp.concatenate([x_ref[g, :, start:], x_ref[g, :, :EDGE]], axis=1)
            else:
                window = x_ref[g, :, start:stop]
            kind = 0 if i == 0 else 2 if i == tiles - 1 else 1
            s_ref[phase, g, :, cols] = mul(window, wk_ref[kind]).astype(bf16)

    def send_halo(phase, g):
        return (
            push(
                s_ref.at[phase, g], hp_ref.at[phase, g], h_send.at[phase, g, 0],
                h_recv.at[phase, g, 0], m, at_band(1),
            ),
            push(
                s_ref.at[phase, g], hn_ref.at[phase, g], h_send.at[phase, g, 1],
                h_recv.at[phase, g, 1], m, at_band(bands - 1),
            ),
        )

    def small_of(g):
        return slice(g * small, (g + 1) * small)

    def large_of(g):
        return slice(g * large, (g + 1) * large)

    def stacked(phase, g, cols):
        return jnp.concatenate(
            [hp_ref[phase, g, :, cols], s_ref[phase, g, :, cols], hn_ref[phase, g, :, cols]],
            axis=0,
        )

    def fold(g, field):
        for cols in every:
            products = (ens_ref[large_of(g), cols] * field(g, cols)).reshape(each, eight, TILE)
            both = (products + pltpu.roll(products, rows, 1)) * scaled
            both = both.reshape(large, TILE).astype(bf16)
            x_ref[g, :, cols] = mul(sel_ref[...], both).astype(bf16)

    def squares(a, b):
        product = a * b
        return jnp.sum(product.reshape(product.shape[0] // 8, 8, TILE), axis=0)

    def pair_copy(stage, g):
        return pltpu.make_async_remote_copy(
            src_ref=part_ref.at[stage, g * each : (g + 1) * each],
            dst_ref=pair_ref.at[stage, g],
            send_sem=pair_send.at[stage, g], recv_sem=pair_recv.at[stage, g],
            device_id=(partner, band), device_id_type=MESH,
        )

    def sum_copy(stage, g, o):
        there = lax.rem(my_place + o, each)
        return pltpu.make_async_remote_copy(
            src_ref=sum_ref.at[stage, g * each + there], dst_ref=rs_ref.at[stage, chip],
            send_sem=rs_send.at[stage, g * each + o], recv_sem=rs_recv.at[stage, chip],
            device_id=(there * groups + g, band), device_id_type=MESH,
        )

    def forward(stage, g):
        @pl.when(core == g % 2)
        def _():
            pair_copy(stage, g).wait_recv()
            span = slice(g * each, (g + 1) * each)
            for cols in every:
                sum_ref[stage, span, :, cols] = (
                    part_ref[stage, span, :, cols].astype(f32)
                    + pair_ref[stage, g, :, :, cols].astype(f32)
                ).astype(bf16)
            for o in range(1, each):
                sum_copy(stage, g, o).start()
            pl.when(my_group != g)(sum_copy(stage, g, 0).start)

            @pl.when(my_group == g)
            def _():
                rs_ref[stage, chip] = sum_ref[stage, place(m)]

    def settle(stage, g):
        pl.when(core != g % 2)(pair_copy(stage, g).wait_send)

        @pl.when(core == g % 2)
        def _():
            for o in range(1, each):
                sum_copy(stage, g, o).wait_send()
            pl.when(my_group != g)(sum_copy(stage, g, 0).wait_send)

    def image(phase, stage, static_ref, out, halos):
        def static(cols):
            out[:, cols] = static_share * mul_wide(krm_ref, static_ref[:, cols])

        over_tiles(static)
        for g in range(groups):
            for copy in halos[g]:
                copy.wait_recv()
            for cols in every:
                localized = mul(t2_ref[large_of(g)], stacked(phase, g, cols))
                products = localized * c2_ref[large_of(g), 0:1] * ens_ref[large_of(g), cols]
                part_ref[stage, g * each : (g + 1) * each, :, cols] = products.reshape(
                    each, eight, TILE
                ).astype(bf16)
            if g > 0:
                forward(stage, g - 1)
            pl.when(core != g % 2)(pair_copy(stage, g).start)
        forward(stage, groups - 1)
        for o in range(1, chips):
            source = lax.rem(chip + chips - o, chips)
            arrived(
                sum_ref.at[stage, 0], rs_ref.at[stage, source], rs_send.at[stage, 0],
                rs_recv.at[stage, source], at_m(2 * o), band,
            )

        def collect(cols):
            out[:, cols] = out[:, cols] + jnp.sum(rs_ref[stage, :, :, cols].astype(f32), axis=0)

        over_tiles(collect)

    def total_of(acc):
        return jnp.sum(jnp.sum(acc, axis=1, keepdims=True), axis=0, keepdims=True)

    def pack(values):
        line = iota((8, 128), 0)
        packed = jnp.zeros((8, 128), f32)
        for at, value in enumerate(values):
            packed = jnp.where(line == at, value, packed)
        return packed

    def gather_start(k, stage, value, table, count, own, peer, send, recv):
        vec_ref[k, stage] = value
        table[k, own] = value
        for o in range(1, count):
            member, other = peer(o)
            push(
                vec_ref.at[k, stage], table.at[k, own], send.at[k, o - 1], recv.at[k, o - 1],
                member, other,
            )

    def gather_wait(k, stage, table, count, source, peer, send, recv):
        for o in range(1, count):
            member, other = peer(o)
            arrived(
                vec_ref.at[k, stage], table.at[k, source(o)], send.at[k, o - 1],
                recv.at[k, o - 1], member, other,
            )
        return jnp.sum(table[k], axis=0)

    def m_to(o):
        return at_m(o), band

    def x_to(o):
        return m, by * across + x_peer(o)

    def y_to(o):
        return m, y_peer(o) * across + bx

    def m_start(k, value):
        gather_start(k, 0, value, allm_ref, members, m, m_to, m_send, m_recv)

    def m_wait(k):
        return gather_wait(k, 0, allm_ref, members, lambda o: at_m(members - o), m_to, m_send, m_recv)

    def x_start(k, value):
        gather_start(k, 1, value, allx_ref, across, bx, x_to, x_send, x_recv)

    def x_wait(k):
        return gather_wait(k, 1, allx_ref, across, lambda o: x_peer(across - o), x_to, x_send, x_recv)

    def y_start(k, value):
        gather_start(k, 2, value, ally_ref, up, by, y_to, y_send, y_recv)

    def y_wait(k):
        return gather_wait(k, 2, ally_ref, up, lambda o: y_peer(up - o), y_to, y_send, y_recv)

    halos = []
    for g in range(groups):
        load(g)
        fold(g, lambda g, cols: w0_ref[large_of(g), cols])
        smooth(0, g)
        if g == 0:
            pl.semaphore_wait(barrier, greeted)
        halos.append(send_halo(0, g))

    def first_static(cols, acc):
        value = static_share * mul_wide(krt_ref, w0_ref[:, cols])
        r0s_ref[:, cols] = value
        return acc + squares(value, value)

    precise = prec_ref[m].astype(f32)
    p_ref[:, :width] = jnp.concatenate([precise, precise], axis=0)
    zero = jnp.zeros((8, TILE), f32)
    rr_static = over_tiles(first_static, zero)

    rr_members = zero
    waits, halos = halos, []
    for g in range(groups):
        for copy in waits[g]:
            copy.wait_recv()
        for cols in every:
            value = mul(t1_ref[small_of(g)], stacked(0, g, cols)) * c1_ref[small_of(g), 0:1]
            r0_ref[small_of(g), cols] = value
            x_ref[g, :, cols] = value.astype(bf16)
            rr_members = rr_members + squares(value, value)
        smooth(1, g)
        halos.append(send_halo(1, g))
    image(1, 0, r0s_ref, im0_ref, halos)

    def weigh(cols, acc):
        value = im0_ref[:, cols]
        weighted = p_ref[:, cols] * value
        gown_ref[:, cols] = weighted.astype(bf16)
        return acc + weighted * value

    q00 = over_tiles(weigh, zero)
    gall_ref[place(m)] = gown_ref[...]
    m_start(0, pack([total_of(rr_members + rr_static * (1.0 / members)), total_of(q00)]))
    order = sorted(range(1, chips), key=lambda o: min(o, chips - o))
    for o in order[::-1]:
        push(gown_ref, gall_ref.at[place(m)], g_send.at[o], g_recv.at[m], at_m(2 * o), band)
    push(gown_ref, gall_ref.at[place(m)], g_send.at[0], g_recv.at[m], partner, band)
    x_start(0, m_wait(0))
    for o in order:
        source = at_m(members - 2 * o)
        spot = gall_ref.at[place(source)]
        arrived(gown_ref, spot, g_send.at[o], g_recv.at[source], at_m(2 * o), band)
        push(spot, spot, g_send.at[chips + o], g_recv.at[source], partner, band)
    y_start(0, x_wait(0))
    for o in [0] + order:
        source = lax.rem(partner + members - 2 * o, members)
        spot = gall_ref.at[place(source)]
        arrived(gown_ref, spot, g_send.at[0], g_recv.at[source], partner, band)

    waits = []
    for g in range(groups):
        fold(g, lambda g, cols: gall_ref[g * each : (g + 1) * each, :, cols].astype(f32).reshape(
            large, TILE
        ))
        smooth(2, g)
        waits.append(send_halo(2, g))

    def second_static(cols):
        field = gall_ref[:, :, cols].astype(f32).reshape(rows2, TILE).astype(bf16)
        r1s_ref[:, cols] = r0s_ref[:, cols] + static_share * (
            mul(krt_ref[0], field) + mul(krt_ref[1], field)
        )

    over_tiles(second_static)
    tot_ref[0] = y_wait(0)
    rr0 = tot_ref[0, 0:1, 0:1]
    q00 = tot_ref[0, 1:2, 0:1]
    alpha0 = rr0 / (rr0 + q00)
    rr_members = zero
    cross_members = zero
    halos = []
    for g in range(groups):
        for copy in waits[g]:
            copy.wait_recv()
        for cols in every:
            first = r0_ref[small_of(g), cols]
            localized = mul(t1_ref[small_of(g)], stacked(2, g, cols)) * c1_ref[small_of(g), 0:1]
            value = first - alpha0 * (first + localized)
            r1_ref[small_of(g), cols] = value
            x_ref[g, :, cols] = value.astype(bf16)
            rr_members = rr_members + squares(value, value)
            cross_members = cross_members + squares(value, first)
        smooth(3, g)
        halos.append(send_halo(3, g))

    def second_static_residual(cols, acc):
        rr, cross = acc
        first = r0s_ref[:, cols]
        value = first - alpha0 * r1s_ref[:, cols]
        r1s_ref[:, cols] = value
        return rr + squares(value, value), cross + squares(value, first)

    rr_static, cross_static = over_tiles(second_static_residual, (zero, zero))
    image(3, 1, r1s_ref, im1_ref, halos)

    def second_sums(cols, acc):
        q11, q01 = acc
        value = im1_ref[:, cols]
        weighted = p_ref[:, cols] * value
        return q11 + weighted * value, q01 + weighted * im0_ref[:, cols]

    q11, q01 = over_tiles(second_sums, (zero, zero))
    share = 1.0 / members
    m_start(1, pack([
        total_of(rr_members + rr_static * share),
        total_of(cross_members + cross_static * share),
        total_of(q11),
        total_of(q01),
    ]))
    x_start(1, m_wait(1))
    y_start(1, x_wait(1))
    tot_ref[1] = y_wait(1)
    rr1 = tot_ref[1, 0:1, 0:1]
    cross = tot_ref[1, 1:2, 0:1]
    q11 = tot_ref[1, 2:3, 0:1]
    q01 = tot_ref[1, 3:4, 0:1]
    beta = rr1 / rr0
    length = rr1 + beta * (2.0 * cross + beta * rr0)
    curvature = length + q11 + beta * (2.0 * q01 + beta * q00)
    alpha1 = rr1 / curvature
    ahead = alpha0 + alpha1 * beta

    def blend(first, second, lines):
        return ahead * first[lines, :width] + alpha1 * second[lines, :width]

    for start in range(0, rows1, eight):
        lines = slice(start, start + eight)
        members_out = blend(r0_ref, r1_ref, lines)
        static_out = blend(r0s_ref, r1s_ref, lines)
        for at in range(2):
            line = start // rows + at
            level = line % each * groups + line // each
            outm_ref[0, level] = members_out[at * rows : (at + 1) * rows]
            outs_ref[level] = static_out[at * rows : (at + 1) * rows]
    increment = blend(im0_ref, im1_ref, slice(0, eight))
    for t in range(2):
        inc_ref[t, 0] = increment[t * rows : (t + 1) * rows]
    for copy in sends:
        copy.wait_send()
    for stage in range(2):
        for g in range(groups):
            settle(stage, g)


def shards(ensemble, member_weight, member_of_slot, halfwidth, static_root, innovation, precision):
    f32, bf16 = jnp.float32, jnp.bfloat16
    _, slots, levels, rows, width = ensemble.shape
    members = lax.axis_size("member")
    bands = lax.axis_size("band")
    across = 4 if bands % 4 == 0 else 1
    up = bands // across
    groups = max(levels // 4, 1)
    each = levels // groups
    padded = -(-width // TILE) * TILE
    tiles = padded // TILE
    eight = slots * rows
    rows1, rows2 = levels * rows, levels * eight
    small, large = each * rows, each * eight

    weights = jnp.asarray(window_weights(width, padded), bf16)

    vmem = pl.BlockSpec(memory_space=pltpu.VMEM)
    smem = pl.BlockSpec(memory_space=pltpu.SMEM)
    dma = pltpu.SemaphoreType.DMA
    return pl.pallas_call(
        functools.partial(kernel, members, bands, across, tiles, groups),
        out_shape=[
            jax.ShapeDtypeStruct((1, levels, rows, width), f32),
            jax.ShapeDtypeStruct((levels, rows, width), f32),
            jax.ShapeDtypeStruct((slots, 1, rows, width), f32),
        ],
        in_specs=[smem] * 3 + [vmem] * 5,
        out_specs=[vmem] * 3,
        scratch_shapes=[
            pltpu.VMEM((rows2, padded), f32),
            pltpu.VMEM((rows2, padded), f32),
            pltpu.VMEM((eight, padded), f32),
            pltpu.VMEM((rows1, 3 * small), bf16),
            pltpu.VMEM((rows2, 3 * small), bf16),
            pltpu.VMEM((rows1, 128), f32),
            pltpu.VMEM((rows2, 128), f32),
            pltpu.VMEM((small, large), bf16),
            pltpu.VMEM((2, rows1, rows2), bf16),
            pltpu.VMEM((2, eight, rows1), bf16),
            pltpu.VMEM((groups, small, padded), bf16),
            pltpu.VMEM((4, groups, small, padded), bf16),
            pltpu.VMEM((4, groups, small, padded), bf16),
            pltpu.VMEM((4, groups, small, padded), bf16),
            pltpu.VMEM((2, levels, eight, padded), bf16),
            pltpu.VMEM((2, groups, each, eight, padded), bf16),
            pltpu.VMEM((2, levels, eight, padded), bf16),
            pltpu.VMEM((2, members // 2, eight, padded), bf16),
            pltpu.VMEM((eight, padded), bf16),
            pltpu.VMEM((levels, eight, padded), bf16),
            pltpu.VMEM((rows1, padded), f32),
            pltpu.VMEM((rows1, padded), f32),
            pltpu.VMEM((rows1, padded), f32),
            pltpu.VMEM((rows1, padded), f32),
            pltpu.VMEM((eight, padded), f32),
            pltpu.VMEM((eight, padded), f32),
            pltpu.VMEM((2, 3, 8, 128), f32),
            pltpu.VMEM((2, 8, 128), f32),
            pltpu.VMEM((2, members, 8, 128), f32),
            pltpu.VMEM((2, across, 8, 128), f32),
            pltpu.VMEM((2, up, 8, 128), f32),
            dma((4, groups, 2)),
            dma((4, groups, 2)),
            dma((2, groups)),
            dma((2, groups)),
            dma((2, members)),
            dma((2, members // 2)),
            dma((members,)),
            dma((members,)),
            dma((2, members - 1)),
            dma((2, members - 1)),
            dma((2, max(across - 1, 1))),
            dma((2, max(across - 1, 1))),
            dma((2, max(up - 1, 1))),
            dma((2, max(up - 1, 1))),
        ],
        compiler_params=pltpu.CompilerParams(collective_id=0, has_side_effects=True),
    )(
        member_weight, member_of_slot, halfwidth, ensemble, innovation, precision,
        static_root, weights,
    )


def solution(mesh):
    return jax.shard_map(
        shards,
        mesh=mesh,
        in_specs=(
            P("member", None, None, "band", None),
            P(),
            P("member"),
            P(),
            P(),
            P(None, None, "band", None),
            P(None, "band", None),
        ),
        out_specs=(
            P("member", None, "band", None),
            P(None, "band", None),
            P(None, "member", "band", None),
        ),
        check_vma=False,
    )
```

```python
import functools
import math

import jax
import jax.numpy as jnp
import numpy as np
from jax import lax
from jax.experimental import pallas as pl
from jax.experimental.pallas import tpu as pltpu
from jax.sharding import PartitionSpec as P

HMAX = 4
LREACH = 18
TILE = 256
EDGE = 128

ensemble_share = 0.8
static_share = 0.6
length_scale = 6.0
MESH = pl.DeviceIdType.MESH


def window_weights(width, padded):
    tiles = padded // TILE
    kinds = []
    for tile in (0, 1, tiles - 1):
        start = tile * TILE
        rows = np.arange(start - EDGE, start + TILE + EDGE)
        if tile == 0:
            rows[:EDGE] = np.arange(padded - EDGE, padded)
        if tile == tiles - 1:
            rows[-EDGE:] = np.arange(EDGE)
        cols = np.arange(start, start + TILE)
        apart = np.abs(rows[:, None] - cols[None, :])
        apart = np.minimum(apart, width - apart)
        near = (apart <= LREACH) & (rows[:, None] < width) & (cols[None, :] < width)
        distance = apart.astype(np.float32)
        values = np.exp(-0.5 * (distance / np.float32(length_scale)) ** 2) / np.float32(
            length_scale * math.sqrt(2.0 * math.pi)
        )
        kinds.append(np.where(near, values, 0.0).astype(np.float32))
    return np.stack(kinds)


def mul(a, b):
    return jnp.dot(a, b, preferred_element_type=jnp.float32)


def mul_wide(weights, field):
    high = field.astype(jnp.bfloat16)
    low = (field - high.astype(jnp.float32)).astype(jnp.bfloat16)
    return mul(weights[0], high) + mul(weights[0], low) + mul(weights[1], high)


def kernel(
    members, bands, tiles, groups,
    weight_ref, slot_ref, half_ref,
    raw_hbm, innov_hbm, prec_hbm, root_hbm, wk_hbm,
    outm_ref, outs_ref, inc_ref,
    raw_ref, innov_ref, prec_ref, root_ref, wk_ref, in_sem,
    ens_ref, w0_ref, p_ref,
    t1_ref, t2_ref, c1_ref, c2_ref, sel_ref, krt_ref, krm_ref,
    x_ref, s_ref, hp_ref, hn_ref, part_ref, pair_ref, sum_ref, rs_ref, gown_ref, gall_ref,
    r0_ref, r1_ref, r0s_ref, r1s_ref, im0_ref, im1_ref,
    vec_ref, tot_ref, allm_ref, allb_ref,
    h_send, h_recv, pair_send, pair_recv, rs_send, rs_recv, g_send, g_recv, m_send, m_recv, b_send, b_recv,
):
    f32, bf16 = jnp.float32, jnp.bfloat16
    m = lax.axis_index("member")
    band = lax.axis_index("band")
    levels, eight = gall_ref.shape[0], gall_ref.shape[1]
    rows = eight // 2
    rows1, rows2 = levels * rows, levels * eight
    each = levels // groups
    small, large = each * rows, each * eight
    chips = members // 2
    core = lax.rem(m, 2)
    chip = m // 2
    partner = m + 1 - 2 * core
    my_group = lax.rem(m, groups)
    my_place = m // groups

    def at_m(o):
        return lax.rem(m + o, members)

    def at_band(o):
        return lax.rem(band + o, bands)

    def place(level):
        return lax.rem(level, groups) * each + level // groups

    fetches = [
        pltpu.make_async_copy(src, dst, in_sem.at[at])
        for at, (src, dst) in enumerate([
            (root_hbm, root_ref), (raw_hbm, raw_ref), (innov_hbm, innov_ref),
            (prec_hbm, prec_ref), (wk_hbm, wk_ref),
        ])
    ]
    for fetch in fetches:
        fetch.start()
    barrier = pltpu.get_barrier_semaphore()
    greeted = 0
    for o in range(1, members):
        pl.semaphore_signal(
            barrier, inc=1, device_id=(at_m(o), band), device_id_type=MESH
        )
        greeted += 1
    others = [at_band(o) for o in range(1, bands)]
    for other in others:
        pl.semaphore_signal(barrier, inc=1, device_id=(m, other), device_id_type=MESH)
        greeted += 1

    def iota(shape, axis):
        return lax.broadcasted_iota(jnp.int32, shape, axis)

    def over(index, size):
        return lax.shift_right_logical(index, size.bit_length() - 1)

    def level_of(index, height):
        inside = index & (each * height - 1)
        return over(inside, height) * groups + over(index, each * height)

    def span_of(level):
        span = jnp.zeros(level.shape, jnp.int32)
        for at in range(levels):
            span = jnp.where(level == at, half_ref[at] + 1, span)
        return span

    low_side = jnp.where(band > 0, 1, 0)
    high_side = jnp.where(band < bands - 1, 1, 0)
    scaled = jnp.float32(0.0)
    for at in range(members):
        scaled = scaled + jnp.where(slot_ref[0] == at, weight_ref[at], 0.0)

    def taper(height, out, factors, extra):
        shape = (levels * height, 3 * small)
        line, col = iota(shape, 0), iota(shape, 1)
        side = jnp.where(col >= small, 1, 0) + jnp.where(col >= 2 * small, 1, 0)
        within = col - side * small
        apart = jnp.abs((within & (rows - 1)) + (side - 1) * rows - (line & (rows - 1)))
        same = over(within, rows) == over(line & (each * height - 1), height)
        seen = jnp.where(side == 0, low_side, jnp.where(side == 2, high_side, 1)) == 1
        span = span_of(level_of(line, height))
        values = jnp.where(same & seen, jnp.maximum(span - apart, 0), 0)
        out[...] = values.astype(f32).astype(bf16)
        spans = span_of(level_of(iota(factors.shape, 0), height)).astype(f32)
        factors[...] = extra / (spans * spans)

    taper(rows, t1_ref, c1_ref, ensemble_share)
    taper(eight, t2_ref, c2_ref, ensemble_share * scaled)

    def ones(condition):
        return jnp.where(condition, 1.0, 0.0).astype(f32)

    line, col = iota((small, large), 0), iota((small, large), 1)
    picked = over(line, rows) * eight + (line & (rows - 1))
    sel_ref[...] = ones(col == picked).astype(bf16)
    shape = (rows1, levels)
    place1 = ones(level_of(iota(shape, 0), rows) == iota(shape, 1)).astype(bf16)
    shape = (levels, rows2)
    level2 = ones(level_of(iota(shape, 1), eight) == iota(shape, 0)).astype(bf16)
    shape = (levels, rows1)
    level1 = ones(level_of(iota(shape, 1), rows) == iota(shape, 0)).astype(bf16)
    shape = (eight, levels)
    mine = ones(iota(shape, 1) == m).astype(bf16)
    shape = (rows1, rows2)
    match = ones((iota(shape, 0) & (rows - 1)) == (iota(shape, 1) & (rows - 1)))
    shape = (eight, rows1)
    match_row = ones((iota(shape, 0) & (rows - 1)) == (iota(shape, 1) & (rows - 1)))
    for fetch in fetches:
        fetch.wait()

    root = root_ref[...]
    root_high = root.astype(bf16)
    root_low = (root - root_high.astype(f32)).astype(bf16)
    for at, piece in enumerate((root_high, root_low)):
        spread = lax.dot_general(
            place1, piece, (((1,), (1,)), ((), ())), preferred_element_type=f32
        )
        krt_ref[at] = (mul(spread.astype(bf16), level2) * match).astype(bf16)
        spread = mul(mine, piece)
        krm_ref[at] = (mul(spread.astype(bf16), level1) * match_row).astype(bf16)

    width = prec_ref.shape[2]
    for target in (ens_ref, w0_ref, p_ref):
        target[:, width - width % 128 :] = jnp.zeros(
            (target.shape[0], target.shape[1] - width + width % 128), f32
        )

    def load(g):
        for j in range(each):
            level = j * groups + g
            lines = slice((g * each + j) * eight, (g * each + j + 1) * eight)
            precise = prec_ref[level].astype(f32)
            ens_ref[lines, :width] = jnp.concatenate(
                [raw_ref[0, t, level].astype(f32) for t in range(2)], axis=0
            )
            w0_ref[lines, :width] = jnp.concatenate(
                [innov_ref[t, level].astype(f32) * precise for t in range(2)], axis=0
            )

    sends = []

    def push(src, dst, send, recv, member, other):
        copy = pltpu.make_async_remote_copy(
            src_ref=src, dst_ref=dst, send_sem=send, recv_sem=recv,
            device_id=(member, other), device_id_type=MESH,
        )
        copy.start()
        sends.append(copy)
        return copy

    def arrived(like, dst, send, recv, member, other):
        pltpu.make_async_remote_copy(
            src_ref=like, dst_ref=dst, send_sem=send, recv_sem=recv,
            device_id=(member, other), device_id_type=MESH,
        ).wait_recv()

    def columns(i):
        return pl.ds(pl.multiple_of(i * TILE, TILE), TILE)

    def over_tiles(body, init=None):
        if init is None:
            def step(i, carry):
                body(columns(i))
                return carry
            lax.fori_loop(0, tiles, step, 0)
            return None
        return lax.fori_loop(0, tiles, lambda i, carry: body(columns(i), carry), init)

    every = [slice(i * TILE, (i + 1) * TILE) for i in range(tiles)]
    last = tiles * TILE

    def smooth(phase, g):
        for i, cols in enumerate(every):
            start, stop = i * TILE - EDGE, (i + 1) * TILE + EDGE
            if i == 0:
                window = jnp.concatenate([x_ref[g, :, last - EDGE :], x_ref[g, :, :stop]], axis=1)
            elif i == tiles - 1:
                window = jnp.concatenate([x_ref[g, :, start:], x_ref[g, :, :EDGE]], axis=1)
            else:
                window = x_ref[g, :, start:stop]
            kind = 0 if i == 0 else 2 if i == tiles - 1 else 1
            s_ref[phase, g, :, cols] = mul(window, wk_ref[kind]).astype(bf16)

    def send_halo(phase, g):
        return (
            push(
                s_ref.at[phase, g], hp_ref.at[phase, g], h_send.at[phase, g, 0],
                h_recv.at[phase, g, 0], m, at_band(1),
            ),
            push(
                s_ref.at[phase, g], hn_ref.at[phase, g], h_send.at[phase, g, 1],
                h_recv.at[phase, g, 1], m, at_band(bands - 1),
            ),
        )

    def small_of(g):
        return slice(g * small, (g + 1) * small)

    def large_of(g):
        return slice(g * large, (g + 1) * large)

    def stacked(phase, g, cols):
        return jnp.concatenate(
            [hp_ref[phase, g, :, cols], s_ref[phase, g, :, cols], hn_ref[phase, g, :, cols]],
            axis=0,
        )

    def fold(g, field):
        for cols in every:
            products = (ens_ref[large_of(g), cols] * field(g, cols)).reshape(each, eight, TILE)
            both = (products + pltpu.roll(products, rows, 1)) * scaled
            both = both.reshape(large, TILE).astype(bf16)
            x_ref[g, :, cols] = mul(sel_ref[...], both).astype(bf16)

    def squares(a, b):
        product = a * b
        return jnp.sum(product.reshape(product.shape[0] // 8, 8, TILE), axis=0)

    def pair_copy(stage, g):
        return pltpu.make_async_remote_copy(
            src_ref=part_ref.at[stage, g * each : (g + 1) * each],
            dst_ref=pair_ref.at[stage, g],
            send_sem=pair_send.at[stage, g], recv_sem=pair_recv.at[stage, g],
            device_id=(partner, band), device_id_type=MESH,
        )

    def sum_copy(stage, g, o):
        there = lax.rem(my_place + o, each)
        return pltpu.make_async_remote_copy(
            src_ref=sum_ref.at[stage, g * each + there], dst_ref=rs_ref.at[stage, chip],
            send_sem=rs_send.at[stage, g * each + o], recv_sem=rs_recv.at[stage, chip],
            device_id=(there * groups + g, band), device_id_type=MESH,
        )

    def forward(stage, g):
        @pl.when(core == g % 2)
        def _():
            pair_copy(stage, g).wait_recv()
            span = slice(g * each, (g + 1) * each)
            for cols in every:
                sum_ref[stage, span, :, cols] = (
                    part_ref[stage, span, :, cols].astype(f32)
                    + pair_ref[stage, g, :, :, cols].astype(f32)
                ).astype(bf16)
            for o in range(1, each):
                sum_copy(stage, g, o).start()
            pl.when(my_group != g)(sum_copy(stage, g, 0).start)

            @pl.when(my_group == g)
            def _():
                rs_ref[stage, chip] = sum_ref[stage, place(m)]

    def settle(stage, g):
        pl.when(core != g % 2)(pair_copy(stage, g).wait_send)

        @pl.when(core == g % 2)
        def _():
            for o in range(1, each):
                sum_copy(stage, g, o).wait_send()
            pl.when(my_group != g)(sum_copy(stage, g, 0).wait_send)

    def image(phase, stage, static_ref, out, halos):
        def static(cols):
            out[:, cols] = static_share * mul_wide(krm_ref, static_ref[:, cols])

        over_tiles(static)
        for g in range(groups):
            for copy in halos[g]:
                copy.wait_recv()
            for cols in every:
                localized = mul(t2_ref[large_of(g)], stacked(phase, g, cols))
                products = localized * c2_ref[large_of(g), 0:1] * ens_ref[large_of(g), cols]
                part_ref[stage, g * each : (g + 1) * each, :, cols] = products.reshape(
                    each, eight, TILE
                ).astype(bf16)
            if g > 0:
                forward(stage, g - 1)
            pl.when(core != g % 2)(pair_copy(stage, g).start)
        forward(stage, groups - 1)
        for o in range(1, chips):
            source = lax.rem(chip + chips - o, chips)
            arrived(
                sum_ref.at[stage, 0], rs_ref.at[stage, source], rs_send.at[stage, 0],
                rs_recv.at[stage, source], at_m(2 * o), band,
            )

        def collect(cols):
            out[:, cols] = out[:, cols] + jnp.sum(rs_ref[stage, :, :, cols].astype(f32), axis=0)

        over_tiles(collect)

    def total_of(acc):
        return jnp.sum(jnp.sum(acc, axis=1, keepdims=True), axis=0, keepdims=True)

    def pack(values):
        line = iota((8, 128), 0)
        packed = jnp.zeros((8, 128), f32)
        for at, value in enumerate(values):
            packed = jnp.where(line == at, value, packed)
        return packed

    def gather_start(k, stage, value, table, count, own, peer, send, recv):
        vec_ref[k, stage] = value
        table[k, own] = value
        for o in range(1, count):
            member, other = peer(o)
            push(
                vec_ref.at[k, stage], table.at[k, own], send.at[k, o - 1], recv.at[k, o - 1],
                member, other,
            )

    def gather_wait(k, stage, table, count, source, peer, send, recv):
        for o in range(1, count):
            member, other = peer(o)
            arrived(
                vec_ref.at[k, stage], table.at[k, source(o)], send.at[k, o - 1],
                recv.at[k, o - 1], member, other,
            )
        return jnp.sum(table[k], axis=0)

    def m_to(o):
        return at_m(o), band

    def b_to(o):
        return m, at_band(o)

    def m_start(k, value):
        gather_start(k, 0, value, allm_ref, members, m, m_to, m_send, m_recv)

    def m_wait(k):
        return gather_wait(k, 0, allm_ref, members, lambda o: at_m(members - o), m_to, m_send, m_recv)

    def b_start(k, value):
        gather_start(k, 1, value, allb_ref, bands, band, b_to, b_send, b_recv)

    def b_wait(k):
        return gather_wait(
            k, 1, allb_ref, bands, lambda o: at_band(bands - o), b_to, b_send, b_recv
        )

    halos = []
    for g in range(groups):
        load(g)
        fold(g, lambda g, cols: w0_ref[large_of(g), cols])
        smooth(0, g)
        if g == 0:
            pl.semaphore_wait(barrier, greeted)
        halos.append(send_halo(0, g))

    def first_static(cols, acc):
        value = static_share * mul_wide(krt_ref, w0_ref[:, cols])
        r0s_ref[:, cols] = value
        return acc + squares(value, value)

    precise = prec_ref[m].astype(f32)
    p_ref[:, :width] = jnp.concatenate([precise, precise], axis=0)
    zero = jnp.zeros((8, TILE), f32)
    rr_static = over_tiles(first_static, zero)

    rr_members = zero
    waits, halos = halos, []
    for g in range(groups):
        for copy in waits[g]:
            copy.wait_recv()
        for cols in every:
            value = mul(t1_ref[small_of(g)], stacked(0, g, cols)) * c1_ref[small_of(g), 0:1]
            r0_ref[small_of(g), cols] = value
            x_ref[g, :, cols] = value.astype(bf16)
            rr_members = rr_members + squares(value, value)
        smooth(1, g)
        halos.append(send_halo(1, g))
    image(1, 0, r0s_ref, im0_ref, halos)

    def weigh(cols, acc):
        value = im0_ref[:, cols]
        weighted = p_ref[:, cols] * value
        gown_ref[:, cols] = weighted.astype(bf16)
        return acc + weighted * value

    q00 = over_tiles(weigh, zero)
    gall_ref[place(m)] = gown_ref[...]
    m_start(0, pack([total_of(rr_members + rr_static * (1.0 / members)), total_of(q00)]))
    order = sorted(range(1, chips), key=lambda o: min(o, chips - o))
    for o in order[::-1]:
        push(gown_ref, gall_ref.at[place(m)], g_send.at[o], g_recv.at[m], at_m(2 * o), band)
    push(gown_ref, gall_ref.at[place(m)], g_send.at[0], g_recv.at[m], partner, band)
    b_start(0, m_wait(0))
    for o in order:
        source = at_m(members - 2 * o)
        spot = gall_ref.at[place(source)]
        arrived(gown_ref, spot, g_send.at[o], g_recv.at[source], at_m(2 * o), band)
        push(spot, spot, g_send.at[chips + o], g_recv.at[source], partner, band)
    for o in [0] + order:
        source = lax.rem(partner + members - 2 * o, members)
        spot = gall_ref.at[place(source)]
        arrived(gown_ref, spot, g_send.at[0], g_recv.at[source], partner, band)

    waits = []
    for g in range(groups):
        fold(g, lambda g, cols: gall_ref[g * each : (g + 1) * each, :, cols].astype(f32).reshape(
            large, TILE
        ))
        smooth(2, g)
        waits.append(send_halo(2, g))

    def second_static(cols):
        field = gall_ref[:, :, cols].astype(f32).reshape(rows2, TILE).astype(bf16)
        r1s_ref[:, cols] = r0s_ref[:, cols] + static_share * (
            mul(krt_ref[0], field) + mul(krt_ref[1], field)
        )

    over_tiles(second_static)
    tot_ref[0] = b_wait(0)
    rr0 = tot_ref[0, 0:1, 0:1]
    q00 = tot_ref[0, 1:2, 0:1]
    alpha0 = rr0 / (rr0 + q00)
    rr_members = zero
    cross_members = zero
    halos = []
    for g in range(groups):
        for copy in waits[g]:
            copy.wait_recv()
        for cols in every:
            first = r0_ref[small_of(g), cols]
            localized = mul(t1_ref[small_of(g)], stacked(2, g, cols)) * c1_ref[small_of(g), 0:1]
            value = first - alpha0 * (first + localized)
            r1_ref[small_of(g), cols] = value
            x_ref[g, :, cols] = value.astype(bf16)
            rr_members = rr_members + squares(value, value)
            cross_members = cross_members + squares(value, first)
        smooth(3, g)
        halos.append(send_halo(3, g))

    def second_static_residual(cols, acc):
        rr, cross = acc
        first = r0s_ref[:, cols]
        value = first - alpha0 * r1s_ref[:, cols]
        r1s_ref[:, cols] = value
        return rr + squares(value, value), cross + squares(value, first)

    rr_static, cross_static = over_tiles(second_static_residual, (zero, zero))
    image(3, 1, r1s_ref, im1_ref, halos)

    def second_sums(cols, acc):
        q11, q01 = acc
        value = im1_ref[:, cols]
        weighted = p_ref[:, cols] * value
        return q11 + weighted * value, q01 + weighted * im0_ref[:, cols]

    q11, q01 = over_tiles(second_sums, (zero, zero))
    share = 1.0 / members
    m_start(1, pack([
        total_of(rr_members + rr_static * share),
        total_of(cross_members + cross_static * share),
        total_of(q11),
        total_of(q01),
    ]))
    b_start(1, m_wait(1))
    tot_ref[1] = b_wait(1)
    rr1 = tot_ref[1, 0:1, 0:1]
    cross = tot_ref[1, 1:2, 0:1]
    q11 = tot_ref[1, 2:3, 0:1]
    q01 = tot_ref[1, 3:4, 0:1]
    beta = rr1 / rr0
    length = rr1 + beta * (2.0 * cross + beta * rr0)
    curvature = length + q11 + beta * (2.0 * q01 + beta * q00)
    alpha1 = rr1 / curvature
    ahead = alpha0 + alpha1 * beta

    def blend(first, second, lines):
        return ahead * first[lines, :width] + alpha1 * second[lines, :width]

    for start in range(0, rows1, eight):
        lines = slice(start, start + eight)
        members_out = blend(r0_ref, r1_ref, lines)
        static_out = blend(r0s_ref, r1s_ref, lines)
        for at in range(2):
            line = start // rows + at
            level = line % each * groups + line // each
            outm_ref[0, level] = members_out[at * rows : (at + 1) * rows]
            outs_ref[level] = static_out[at * rows : (at + 1) * rows]
    increment = blend(im0_ref, im1_ref, slice(0, eight))
    for t in range(2):
        inc_ref[t, 0] = increment[t * rows : (t + 1) * rows]
    for copy in sends:
        copy.wait_send()
    for stage in range(2):
        for g in range(groups):
            settle(stage, g)


def shards(ensemble, member_weight, member_of_slot, halfwidth, static_root, innovation, precision):
    f32, bf16 = jnp.float32, jnp.bfloat16
    _, slots, levels, rows, width = ensemble.shape
    members = lax.axis_size("member")
    bands = lax.axis_size("band")
    groups = max(levels // 4, 1)
    each = levels // groups
    padded = -(-width // TILE) * TILE
    tiles = padded // TILE
    eight = slots * rows
    rows1, rows2 = levels * rows, levels * eight
    small, large = each * rows, each * eight

    weights = jnp.asarray(window_weights(width, padded), bf16)

    vmem = pl.BlockSpec(memory_space=pltpu.VMEM)
    smem = pl.BlockSpec(memory_space=pltpu.SMEM)
    dma = pltpu.SemaphoreType.DMA
    return pl.pallas_call(
        functools.partial(kernel, members, bands, tiles, groups),
        out_shape=[
            jax.ShapeDtypeStruct((1, levels, rows, width), f32),
            jax.ShapeDtypeStruct((levels, rows, width), f32),
            jax.ShapeDtypeStruct((slots, 1, rows, width), f32),
        ],
        in_specs=[smem] * 3 + [pl.BlockSpec(memory_space=pltpu.HBM)] * 5,
        out_specs=[vmem] * 3,
        scratch_shapes=[
            pltpu.VMEM(ensemble.shape, bf16),
            pltpu.VMEM(innovation.shape, bf16),
            pltpu.VMEM(precision.shape, bf16),
            pltpu.VMEM(static_root.shape, f32),
            pltpu.VMEM(weights.shape, bf16),
            dma((5,)),
            pltpu.VMEM((rows2, padded), f32),
            pltpu.VMEM((rows2, padded), f32),
            pltpu.VMEM((eight, padded), f32),
            pltpu.VMEM((rows1, 3 * small), bf16),
            pltpu.VMEM((rows2, 3 * small), bf16),
            pltpu.VMEM((rows1, 128), f32),
            pltpu.VMEM((rows2, 128), f32),
            pltpu.VMEM((small, large), bf16),
            pltpu.VMEM((2, rows1, rows2), bf16),
            pltpu.VMEM((2, eight, rows1), bf16),
            pltpu.VMEM((groups, small, padded), bf16),
            pltpu.VMEM((4, groups, small, padded), bf16),
            pltpu.VMEM((4, groups, small, padded), bf16),
            pltpu.VMEM((4, groups, small, padded), bf16),
            pltpu.VMEM((2, levels, eight, padded), bf16),
            pltpu.VMEM((2, groups, each, eight, padded), bf16),
            pltpu.VMEM((2, levels, eight, padded), bf16),
            pltpu.VMEM((2, members // 2, eight, padded), bf16),
            pltpu.VMEM((eight, padded), bf16),
            pltpu.VMEM((levels, eight, padded), bf16),
            pltpu.VMEM((rows1, padded), f32),
            pltpu.VMEM((rows1, padded), f32),
            pltpu.VMEM((rows1, padded), f32),
            pltpu.VMEM((rows1, padded), f32),
            pltpu.VMEM((eight, padded), f32),
            pltpu.VMEM((eight, padded), f32),
            pltpu.VMEM((2, 2, 8, 128), f32),
            pltpu.VMEM((2, 8, 128), f32),
            pltpu.VMEM((2, members, 8, 128), f32),
            pltpu.VMEM((2, bands, 8, 128), f32),
            dma((4, groups, 2)),
            dma((4, groups, 2)),
            dma((2, groups)),
            dma((2, groups)),
            dma((2, members)),
            dma((2, members // 2)),
            dma((members,)),
            dma((members,)),
            dma((2, members - 1)),
            dma((2, members - 1)),
            dma((2, bands - 1)),
            dma((2, bands - 1)),
        ],
        compiler_params=pltpu.CompilerParams(collective_id=0, has_side_effects=True),
    )(
        member_weight, member_of_slot, halfwidth, ensemble, innovation, precision,
        static_root, weights,
    )


def solution(mesh):
    return jax.shard_map(
        shards,
        mesh=mesh,
        in_specs=(
            P("member", None, None, "band", None),
            P(),
            P("member"),
            P(),
            P(),
            P(None, None, "band", None),
            P(None, "band", None),
        ),
        out_specs=(
            P("member", None, "band", None),
            P(None, "band", None),
            P(None, "member", "band", None),
        ),
        check_vma=False,
    )
```

```python
import functools
import math

import jax
import jax.numpy as jnp
import numpy as np
from jax import lax
from jax.experimental import pallas as pl
from jax.experimental.pallas import tpu as pltpu
from jax.sharding import PartitionSpec as P

HMAX = 4
LREACH = 18
TILE = 256
EDGE = 128

ensemble_share = 0.8
static_share = 0.6
length_scale = 6.0
MESH = pl.DeviceIdType.MESH


def window_weights(width, padded):
    tiles = padded // TILE
    kinds = []
    for tile in (0, 1, tiles - 1):
        start = tile * TILE
        rows = np.arange(start - EDGE, start + TILE + EDGE)
        if tile == 0:
            rows[:EDGE] = np.arange(padded - EDGE, padded)
        if tile == tiles - 1:
            rows[-EDGE:] = np.arange(EDGE)
        cols = np.arange(start, start + TILE)
        apart = np.abs(rows[:, None] - cols[None, :])
        apart = np.minimum(apart, width - apart)
        near = (apart <= LREACH) & (rows[:, None] < width) & (cols[None, :] < width)
        distance = apart.astype(np.float32)
        values = np.exp(-0.5 * (distance / np.float32(length_scale)) ** 2) / np.float32(
            length_scale * math.sqrt(2.0 * math.pi)
        )
        kinds.append(np.where(near, values, 0.0).astype(np.float32))
    return np.stack(kinds)


def mul(a, b):
    return jnp.dot(a, b, preferred_element_type=jnp.float32)


def mul_wide(weights, field):
    high = field.astype(jnp.bfloat16)
    low = (field - high.astype(jnp.float32)).astype(jnp.bfloat16)
    return mul(weights[0], high) + mul(weights[0], low) + mul(weights[1], high)


def kernel(
    members, bands, across, tiles, groups,
    weight_ref, slot_ref, half_ref,
    raw_hbm, innov_hbm, prec_hbm, root_hbm, wk_hbm,
    outm_ref, outs_ref, inc_ref,
    raw_ref, innov_ref, prec_ref, root_ref, wk_ref, in_sem,
    ens_ref, w0_ref, p_ref,
    t1_ref, t2_ref, c1_ref, c2_ref, sel_ref, krt_ref, krm_ref,
    x_ref, s_ref, hp_ref, hn_ref, part_ref, pair_ref, sum_ref, rs_ref, gown_ref, gall_ref,
    r0_ref, r1_ref, r0s_ref, r1s_ref, im0_ref, im1_ref,
    vec_ref, tot_ref, allm_ref, allx_ref, ally_ref,
    h_send, h_recv, pair_send, pair_recv, rs_send, rs_recv, g_send, g_recv, m_send, m_recv, x_send, x_recv, y_send, y_recv,
):
    f32, bf16 = jnp.float32, jnp.bfloat16
    m = lax.axis_index("member")
    band = lax.axis_index("band")
    up = bands // across
    by = band // across
    bx = lax.rem(band, across)
    levels, eight = gall_ref.shape[0], gall_ref.shape[1]
    rows = eight // 2
    rows1, rows2 = levels * rows, levels * eight
    each = levels // groups
    small, large = each * rows, each * eight
    chips = members // 2
    core = lax.rem(m, 2)
    chip = m // 2
    partner = m + 1 - 2 * core
    my_group = lax.rem(m, groups)
    my_place = m // groups

    def at_m(o):
        return lax.rem(m + o, members)

    def at_band(o):
        return lax.rem(band + o, bands)

    def x_peer(o):
        return lax.rem(bx + o, across)

    def y_peer(o):
        return lax.rem(by + o, up)

    def place(level):
        return lax.rem(level, groups) * each + level // groups

    fetches = [
        pltpu.make_async_copy(src, dst, in_sem.at[at])
        for at, (src, dst) in enumerate([
            (root_hbm, root_ref), (raw_hbm, raw_ref), (innov_hbm, innov_ref),
            (prec_hbm, prec_ref), (wk_hbm, wk_ref),
        ])
    ]
    for fetch in fetches:
        fetch.start()
    barrier = pltpu.get_barrier_semaphore()
    greeted = 0
    for o in range(1, members):
        pl.semaphore_signal(
            barrier, inc=1, device_id=(at_m(o), band), device_id_type=MESH
        )
        greeted += 1
    others = [at_band(1), at_band(bands - 1)]
    others += [by * across + x_peer(o) for o in range(1, across)]
    others += [y_peer(o) * across + bx for o in range(1, up)]
    for other in others:
        pl.semaphore_signal(barrier, inc=1, device_id=(m, other), device_id_type=MESH)
        greeted += 1

    def iota(shape, axis):
        return lax.broadcasted_iota(jnp.int32, shape, axis)

    def over(index, size):
        return lax.shift_right_logical(index, size.bit_length() - 1)

    def level_of(index, height):
        inside = index & (each * height - 1)
        return over(inside, height) * groups + over(index, each * height)

    def span_of(level):
        span = jnp.zeros(level.shape, jnp.int32)
        for at in range(levels):
            span = jnp.where(level == at, half_ref[at] + 1, span)
        return span

    low_side = jnp.where(band > 0, 1, 0)
    high_side = jnp.where(band < bands - 1, 1, 0)
    scaled = jnp.float32(0.0)
    for at in range(members):
        scaled = scaled + jnp.where(slot_ref[0] == at, weight_ref[at], 0.0)

    def taper(height, out, factors, extra):
        shape = (levels * height, 3 * small)
        line, col = iota(shape, 0), iota(shape, 1)
        side = jnp.where(col >= small, 1, 0) + jnp.where(col >= 2 * small, 1, 0)
        within = col - side * small
        apart = jnp.abs((within & (rows - 1)) + (side - 1) * rows - (line & (rows - 1)))
        same = over(within, rows) == over(line & (each * height - 1), height)
        seen = jnp.where(side == 0, low_side, jnp.where(side == 2, high_side, 1)) == 1
        span = span_of(level_of(line, height))
        values = jnp.where(same & seen, jnp.maximum(span - apart, 0), 0)
        out[...] = values.astype(f32).astype(bf16)
        spans = span_of(level_of(iota(factors.shape, 0), height)).astype(f32)
        factors[...] = extra / (spans * spans)

    taper(rows, t1_ref, c1_ref, ensemble_share)
    taper(eight, t2_ref, c2_ref, ensemble_share * scaled)

    def ones(condition):
        return jnp.where(condition, 1.0, 0.0).astype(f32)

    line, col = iota((small, large), 0), iota((small, large), 1)
    picked = over(line, rows) * eight + (line & (rows - 1))
    sel_ref[...] = ones(col == picked).astype(bf16)
    shape = (rows1, levels)
    place1 = ones(level_of(iota(shape, 0), rows) == iota(shape, 1)).astype(bf16)
    shape = (levels, rows2)
    level2 = ones(level_of(iota(shape, 1), eight) == iota(shape, 0)).astype(bf16)
    shape = (levels, rows1)
    level1 = ones(level_of(iota(shape, 1), rows) == iota(shape, 0)).astype(bf16)
    shape = (eight, levels)
    mine = ones(iota(shape, 1) == m).astype(bf16)
    shape = (rows1, rows2)
    match = ones((iota(shape, 0) & (rows - 1)) == (iota(shape, 1) & (rows - 1)))
    shape = (eight, rows1)
    match_row = ones((iota(shape, 0) & (rows - 1)) == (iota(shape, 1) & (rows - 1)))
    for fetch in fetches:
        fetch.wait()
    root = root_ref[...]
    root_high = root.astype(bf16)
    root_low = (root - root_high.astype(f32)).astype(bf16)
    for at, piece in enumerate((root_high, root_low)):
        spread = lax.dot_general(
            place1, piece, (((1,), (1,)), ((), ())), preferred_element_type=f32
        )
        krt_ref[at] = (mul(spread.astype(bf16), level2) * match).astype(bf16)
        spread = mul(mine, piece)
        krm_ref[at] = (mul(spread.astype(bf16), level1) * match_row).astype(bf16)

    width = prec_ref.shape[2]
    for target in (ens_ref, w0_ref, p_ref):
        target[:, width - width % 128 :] = jnp.zeros(
            (target.shape[0], target.shape[1] - width + width % 128), f32
        )

    def load(g):
        for j in range(each):
            level = j * groups + g
            lines = slice((g * each + j) * eight, (g * each + j + 1) * eight)
            precise = prec_ref[level].astype(f32)
            ens_ref[lines, :width] = jnp.concatenate(
                [raw_ref[0, t, level].astype(f32) for t in range(2)], axis=0
            )
            w0_ref[lines, :width] = jnp.concatenate(
                [innov_ref[t, level].astype(f32) * precise for t in range(2)], axis=0
            )

    sends = []

    def push(src, dst, send, recv, member, other):
        copy = pltpu.make_async_remote_copy(
            src_ref=src, dst_ref=dst, send_sem=send, recv_sem=recv,
            device_id=(member, other), device_id_type=MESH,
        )
        copy.start()
        sends.append(copy)
        return copy

    def arrived(like, dst, send, recv, member, other):
        pltpu.make_async_remote_copy(
            src_ref=like, dst_ref=dst, send_sem=send, recv_sem=recv,
            device_id=(member, other), device_id_type=MESH,
        ).wait_recv()

    def columns(i):
        return pl.ds(pl.multiple_of(i * TILE, TILE), TILE)

    def over_tiles(body, init=None):
        if init is None:
            def step(i, carry):
                body(columns(i))
                return carry
            lax.fori_loop(0, tiles, step, 0)
            return None
        return lax.fori_loop(0, tiles, lambda i, carry: body(columns(i), carry), init)

    every = [slice(i * TILE, (i + 1) * TILE) for i in range(tiles)]
    last = tiles * TILE

    def smooth(phase, g):
        for i, cols in enumerate(every):
            start, stop = i * TILE - EDGE, (i + 1) * TILE + EDGE
            if i == 0:
                window = jnp.concatenate([x_ref[g, :, last - EDGE :], x_ref[g, :, :stop]], axis=1)
            elif i == tiles - 1:
                window = jnp.concatenate([x_ref[g, :, start:], x_ref[g, :, :EDGE]], axis=1)
            else:
                window = x_ref[g, :, start:stop]
            kind = 0 if i == 0 else 2 if i == tiles - 1 else 1
            s_ref[phase, g, :, cols] = mul(window, wk_ref[kind]).astype(bf16)

    def send_halo(phase, g):
        return (
            push(
                s_ref.at[phase, g], hp_ref.at[phase, g], h_send.at[phase, g, 0],
                h_recv.at[phase, g, 0], m, at_band(1),
            ),
            push(
                s_ref.at[phase, g], hn_ref.at[phase, g], h_send.at[phase, g, 1],
                h_recv.at[phase, g, 1], m, at_band(bands - 1),
            ),
        )

    def small_of(g):
        return slice(g * small, (g + 1) * small)

    def large_of(g):
        return slice(g * large, (g + 1) * large)

    def stacked(phase, g, cols):
        return jnp.concatenate(
            [hp_ref[phase, g, :, cols], s_ref[phase, g, :, cols], hn_ref[phase, g, :, cols]],
            axis=0,
        )

    def fold(g, field):
        for cols in every:
            products = (ens_ref[large_of(g), cols] * field(g, cols)).reshape(each, eight, TILE)
            both = (products + pltpu.roll(products, rows, 1)) * scaled
            both = both.reshape(large, TILE).astype(bf16)
            x_ref[g, :, cols] = mul(sel_ref[...], both).astype(bf16)

    def squares(a, b):
        product = a * b
        return jnp.sum(product.reshape(product.shape[0] // 8, 8, TILE), axis=0)

    def pair_copy(stage, g):
        return pltpu.make_async_remote_copy(
            src_ref=part_ref.at[stage, g * each : (g + 1) * each],
            dst_ref=pair_ref.at[stage, g],
            send_sem=pair_send.at[stage, g], recv_sem=pair_recv.at[stage, g],
            device_id=(partner, band), device_id_type=MESH,
        )

    def sum_copy(stage, g, o):
        there = lax.rem(my_place + o, each)
        return pltpu.make_async_remote_copy(
            src_ref=sum_ref.at[stage, g * each + there], dst_ref=rs_ref.at[stage, chip],
            send_sem=rs_send.at[stage, g * each + o], recv_sem=rs_recv.at[stage, chip],
            device_id=(there * groups + g, band), device_id_type=MESH,
        )

    def forward(stage, g):
        @pl.when(core == g % 2)
        def _():
            pair_copy(stage, g).wait_recv()
            span = slice(g * each, (g + 1) * each)
            for cols in every:
                sum_ref[stage, span, :, cols] = (
                    part_ref[stage, span, :, cols].astype(f32)
                    + pair_ref[stage, g, :, :, cols].astype(f32)
                ).astype(bf16)
            for o in range(1, each):
                sum_copy(stage, g, o).start()
            pl.when(my_group != g)(sum_copy(stage, g, 0).start)

            @pl.when(my_group == g)
            def _():
                rs_ref[stage, chip] = sum_ref[stage, place(m)]

    def settle(stage, g):
        pl.when(core != g % 2)(pair_copy(stage, g).wait_send)

        @pl.when(core == g % 2)
        def _():
            for o in range(1, each):
                sum_copy(stage, g, o).wait_send()
            pl.when(my_group != g)(sum_copy(stage, g, 0).wait_send)

    def image(phase, stage, static_ref, out, halos):
        def static(cols):
            out[:, cols] = static_share * mul_wide(krm_ref, static_ref[:, cols])

        over_tiles(static)
        for g in range(groups):
            for copy in halos[g]:
                copy.wait_recv()
            for cols in every:
                localized = mul(t2_ref[large_of(g)], stacked(phase, g, cols))
                products = localized * c2_ref[large_of(g), 0:1] * ens_ref[large_of(g), cols]
                part_ref[stage, g * each : (g + 1) * each, :, cols] = products.reshape(
                    each, eight, TILE
                ).astype(bf16)
            if g > 0:
                forward(stage, g - 1)
            pl.when(core != g % 2)(pair_copy(stage, g).start)
        forward(stage, groups - 1)
        for o in range(1, chips):
            source = lax.rem(chip + chips - o, chips)
            arrived(
                sum_ref.at[stage, 0], rs_ref.at[stage, source], rs_send.at[stage, 0],
                rs_recv.at[stage, source], at_m(2 * o), band,
            )

        def collect(cols):
            out[:, cols] = out[:, cols] + jnp.sum(rs_ref[stage, :, :, cols].astype(f32), axis=0)

        over_tiles(collect)

    def total_of(acc):
        return jnp.sum(jnp.sum(acc, axis=1, keepdims=True), axis=0, keepdims=True)

    def pack(values):
        line = iota((8, 128), 0)
        packed = jnp.zeros((8, 128), f32)
        for at, value in enumerate(values):
            packed = jnp.where(line == at, value, packed)
        return packed

    def gather_start(k, stage, value, table, count, own, peer, send, recv):
        vec_ref[k, stage] = value
        table[k, own] = value
        for o in range(1, count):
            member, other = peer(o)
            push(
                vec_ref.at[k, stage], table.at[k, own], send.at[k, o - 1], recv.at[k, o - 1],
                member, other,
            )

    def gather_wait(k, stage, table, count, source, peer, send, recv):
        for o in range(1, count):
            member, other = peer(o)
            arrived(
                vec_ref.at[k, stage], table.at[k, source(o)], send.at[k, o - 1],
                recv.at[k, o - 1], member, other,
            )
        return jnp.sum(table[k], axis=0)

    def m_to(o):
        return at_m(o), band

    def x_to(o):
        return m, by * across + x_peer(o)

    def y_to(o):
        return m, y_peer(o) * across + bx

    def m_start(k, value):
        gather_start(k, 0, value, allm_ref, members, m, m_to, m_send, m_recv)

    def m_wait(k):
        return gather_wait(k, 0, allm_ref, members, lambda o: at_m(members - o), m_to, m_send, m_recv)

    def x_start(k, value):
        gather_start(k, 1, value, allx_ref, across, bx, x_to, x_send, x_recv)

    def x_wait(k):
        return gather_wait(k, 1, allx_ref, across, lambda o: x_peer(across - o), x_to, x_send, x_recv)

    def y_start(k, value):
        gather_start(k, 2, value, ally_ref, up, by, y_to, y_send, y_recv)

    def y_wait(k):
        return gather_wait(k, 2, ally_ref, up, lambda o: y_peer(up - o), y_to, y_send, y_recv)

    halos = []
    for g in range(groups):
        load(g)
        fold(g, lambda g, cols: w0_ref[large_of(g), cols])
        smooth(0, g)
        if g == 0:
            pl.semaphore_wait(barrier, greeted)
        halos.append(send_halo(0, g))

    def first_static(cols, acc):
        value = static_share * mul_wide(krt_ref, w0_ref[:, cols])
        r0s_ref[:, cols] = value
        return acc + squares(value, value)

    precise = prec_ref[m].astype(f32)
    p_ref[:, :width] = jnp.concatenate([precise, precise], axis=0)
    zero = jnp.zeros((8, TILE), f32)
    rr_static = over_tiles(first_static, zero)

    rr_members = zero
    waits, halos = halos, []
    for g in range(groups):
        for copy in waits[g]:
            copy.wait_recv()
        for cols in every:
            value = mul(t1_ref[small_of(g)], stacked(0, g, cols)) * c1_ref[small_of(g), 0:1]
            r0_ref[small_of(g), cols] = value
            x_ref[g, :, cols] = value.astype(bf16)
            rr_members = rr_members + squares(value, value)
        smooth(1, g)
        halos.append(send_halo(1, g))
    image(1, 0, r0s_ref, im0_ref, halos)

    def weigh(cols, acc):
        value = im0_ref[:, cols]
        weighted = p_ref[:, cols] * value
        gown_ref[:, cols] = weighted.astype(bf16)
        return acc + weighted * value

    q00 = over_tiles(weigh, zero)
    gall_ref[place(m)] = gown_ref[...]
    m_start(0, pack([total_of(rr_members + rr_static * (1.0 / members)), total_of(q00)]))
    order = sorted(range(1, chips), key=lambda o: min(o, chips - o))
    for o in order[::-1]:
        push(gown_ref, gall_ref.at[place(m)], g_send.at[o], g_recv.at[m], at_m(2 * o), band)
    push(gown_ref, gall_ref.at[place(m)], g_send.at[0], g_recv.at[m], partner, band)
    x_start(0, m_wait(0))
    for o in order:
        source = at_m(members - 2 * o)
        spot = gall_ref.at[place(source)]
        arrived(gown_ref, spot, g_send.at[o], g_recv.at[source], at_m(2 * o), band)
        push(spot, spot, g_send.at[chips + o], g_recv.at[source], partner, band)
    y_start(0, x_wait(0))
    for o in [0] + order:
        source = lax.rem(partner + members - 2 * o, members)
        spot = gall_ref.at[place(source)]
        arrived(gown_ref, spot, g_send.at[0], g_recv.at[source], partner, band)

    waits = []
    for g in range(groups):
        fold(g, lambda g, cols: gall_ref[g * each : (g + 1) * each, :, cols].astype(f32).reshape(
            large, TILE
        ))
        smooth(2, g)
        waits.append(send_halo(2, g))

    def second_static(cols):
        field = gall_ref[:, :, cols].astype(f32).reshape(rows2, TILE).astype(bf16)
        r1s_ref[:, cols] = r0s_ref[:, cols] + static_share * (
            mul(krt_ref[0], field) + mul(krt_ref[1], field)
        )

    over_tiles(second_static)
    tot_ref[0] = y_wait(0)
    rr0 = tot_ref[0, 0:1, 0:1]
    q00 = tot_ref[0, 1:2, 0:1]
    alpha0 = rr0 / (rr0 + q00)
    rr_members = zero
    cross_members = zero
    halos = []
    for g in range(groups):
        for copy in waits[g]:
            copy.wait_recv()
        for cols in every:
            first = r0_ref[small_of(g), cols]
            localized = mul(t1_ref[small_of(g)], stacked(2, g, cols)) * c1_ref[small_of(g), 0:1]
            value = first - alpha0 * (first + localized)
            r1_ref[small_of(g), cols] = value
            x_ref[g, :, cols] = value.astype(bf16)
            rr_members = rr_members + squares(value, value)
            cross_members = cross_members + squares(value, first)
        smooth(3, g)
        halos.append(send_halo(3, g))

    def second_static_residual(cols, acc):
        rr, cross = acc
        first = r0s_ref[:, cols]
        value = first - alpha0 * r1s_ref[:, cols]
        r1s_ref[:, cols] = value
        return rr + squares(value, value), cross + squares(value, first)

    rr_static, cross_static = over_tiles(second_static_residual, (zero, zero))
    image(3, 1, r1s_ref, im1_ref, halos)

    def second_sums(cols, acc):
        q11, q01 = acc
        value = im1_ref[:, cols]
        weighted = p_ref[:, cols] * value
        return q11 + weighted * value, q01 + weighted * im0_ref[:, cols]

    q11, q01 = over_tiles(second_sums, (zero, zero))
    share = 1.0 / members
    m_start(1, pack([
        total_of(rr_members + rr_static * share),
        total_of(cross_members + cross_static * share),
        total_of(q11),
        total_of(q01),
    ]))
    x_start(1, m_wait(1))
    y_start(1, x_wait(1))
    tot_ref[1] = y_wait(1)
    rr1 = tot_ref[1, 0:1, 0:1]
    cross = tot_ref[1, 1:2, 0:1]
    q11 = tot_ref[1, 2:3, 0:1]
    q01 = tot_ref[1, 3:4, 0:1]
    beta = rr1 / rr0
    length = rr1 + beta * (2.0 * cross + beta * rr0)
    curvature = length + q11 + beta * (2.0 * q01 + beta * q00)
    alpha1 = rr1 / curvature
    ahead = alpha0 + alpha1 * beta

    def blend(first, second, lines):
        return ahead * first[lines, :width] + alpha1 * second[lines, :width]

    for start in range(0, rows1, eight):
        lines = slice(start, start + eight)
        members_out = blend(r0_ref, r1_ref, lines)
        static_out = blend(r0s_ref, r1s_ref, lines)
        for at in range(2):
            line = start // rows + at
            level = line % each * groups + line // each
            outm_ref[0, level] = members_out[at * rows : (at + 1) * rows]
            outs_ref[level] = static_out[at * rows : (at + 1) * rows]
    increment = blend(im0_ref, im1_ref, slice(0, eight))
    for t in range(2):
        inc_ref[t, 0] = increment[t * rows : (t + 1) * rows]
    for copy in sends:
        copy.wait_send()
    for stage in range(2):
        for g in range(groups):
            settle(stage, g)


def shards(ensemble, member_weight, member_of_slot, halfwidth, static_root, innovation, precision):
    f32, bf16 = jnp.float32, jnp.bfloat16
    _, slots, levels, rows, width = ensemble.shape
    members = lax.axis_size("member")
    bands = lax.axis_size("band")
    across = 4 if bands % 4 == 0 else 1
    up = bands // across
    groups = max(levels // 4, 1)
    each = levels // groups
    padded = -(-width // TILE) * TILE
    tiles = padded // TILE
    eight = slots * rows
    rows1, rows2 = levels * rows, levels * eight
    small, large = each * rows, each * eight

    weights = jnp.asarray(window_weights(width, padded), bf16)

    vmem = pl.BlockSpec(memory_space=pltpu.VMEM)
    smem = pl.BlockSpec(memory_space=pltpu.SMEM)
    dma = pltpu.SemaphoreType.DMA
    return pl.pallas_call(
        functools.partial(kernel, members, bands, across, tiles, groups),
        out_shape=[
            jax.ShapeDtypeStruct((1, levels, rows, width), f32),
            jax.ShapeDtypeStruct((levels, rows, width), f32),
            jax.ShapeDtypeStruct((slots, 1, rows, width), f32),
        ],
        in_specs=[smem] * 3 + [pl.BlockSpec(memory_space=pltpu.HBM)] * 5,
        out_specs=[vmem] * 3,
        scratch_shapes=[
            pltpu.VMEM(ensemble.shape, bf16),
            pltpu.VMEM(innovation.shape, bf16),
            pltpu.VMEM(precision.shape, bf16),
            pltpu.VMEM(static_root.shape, f32),
            pltpu.VMEM(weights.shape, bf16),
            dma((5,)),
            pltpu.VMEM((rows2, padded), f32),
            pltpu.VMEM((rows2, padded), f32),
            pltpu.VMEM((eight, padded), f32),
            pltpu.VMEM((rows1, 3 * small), bf16),
            pltpu.VMEM((rows2, 3 * small), bf16),
            pltpu.VMEM((rows1, 128), f32),
            pltpu.VMEM((rows2, 128), f32),
            pltpu.VMEM((small, large), bf16),
            pltpu.VMEM((2, rows1, rows2), bf16),
            pltpu.VMEM((2, eight, rows1), bf16),
            pltpu.VMEM((groups, small, padded), bf16),
            pltpu.VMEM((4, groups, small, padded), bf16),
            pltpu.VMEM((4, groups, small, padded), bf16),
            pltpu.VMEM((4, groups, small, padded), bf16),
            pltpu.VMEM((2, levels, eight, padded), bf16),
            pltpu.VMEM((2, groups, each, eight, padded), bf16),
            pltpu.VMEM((2, levels, eight, padded), bf16),
            pltpu.VMEM((2, members // 2, eight, padded), bf16),
            pltpu.VMEM((eight, padded), bf16),
            pltpu.VMEM((levels, eight, padded), bf16),
            pltpu.VMEM((rows1, padded), f32),
            pltpu.VMEM((rows1, padded), f32),
            pltpu.VMEM((rows1, padded), f32),
            pltpu.VMEM((rows1, padded), f32),
            pltpu.VMEM((eight, padded), f32),
            pltpu.VMEM((eight, padded), f32),
            pltpu.VMEM((2, 3, 8, 128), f32),
            pltpu.VMEM((2, 8, 128), f32),
            pltpu.VMEM((2, members, 8, 128), f32),
            pltpu.VMEM((2, across, 8, 128), f32),
            pltpu.VMEM((2, up, 8, 128), f32),
            dma((4, groups, 2)),
            dma((4, groups, 2)),
            dma((2, groups)),
            dma((2, groups)),
            dma((2, members)),
            dma((2, members // 2)),
            dma((members,)),
            dma((members,)),
            dma((2, members - 1)),
            dma((2, members - 1)),
            dma((2, max(across - 1, 1))),
            dma((2, max(across - 1, 1))),
            dma((2, max(up - 1, 1))),
            dma((2, max(up - 1, 1))),
        ],
        compiler_params=pltpu.CompilerParams(collective_id=0, has_side_effects=True),
    )(
        member_weight, member_of_slot, halfwidth, ensemble, innovation, precision,
        static_root, weights,
    )


def solution(mesh):
    return jax.shard_map(
        shards,
        mesh=mesh,
        in_specs=(
            P("member", None, None, "band", None),
            P(),
            P("member"),
            P(),
            P(),
            P(None, None, "band", None),
            P(None, "band", None),
        ),
        out_specs=(
            P("member", None, "band", None),
            P(None, "band", None),
            P(None, "member", "band", None),
        ),
        check_vma=False,
    )
```
